512 devices in a mesh: row: 8 (over x, y_hi), col: 8 (over y_lo, core), scan: 8 (over z).
Axes of the slice: x: 4, y: 8 (y_hi: 2, y_lo: 4; y = y_hi * 4 + y_lo), z: 8, core: 2. Of those that a mesh axis runs over, the one named last changes fastest.
Arguments:
- object_field: float32 [2, 2, 4096, 4096], P(None, None, 'row', 'col'), may hold values from -6 to 6
- probe_field: float32 [2, 256, 256], replicated, may hold values from -6 to 6
- prop_phase: float32 [256, 256], replicated, may hold values from -3.140625 to 3.140625
- measured: float32 [8, 8, 8, 3, 256, 256], P('row', 'col', 'scan'), may hold values from 0.3 to 3
- positions: int32 [8, 8, 8, 3, 2], P('row', 'col', 'scan'), may hold values from -64 to 320, as said below
- counts: int32 [8, 8, 8], P('row', 'col', 'scan'), may hold values from 1 to 3, as said below
Outputs:
- object_grad: float32 [2, 2, 4096, 4096], P(None, None, ('row', 'scan'), 'col')
The draws below stay inside these ranges and needn't reach their ends.
Inputs may be any that keep to these rules, and one draw needn't show every extreme that they name: `positions`: every patch lies inside the object; slots at and past the device's count are unused. `counts`: loads are uneven: some devices hold 3 patches while others of the same tile hold one.
All inputs are finite; a program needn't handle non-finite values.
Results may differ from the reference program's by a relative error of at most 0.018.
Values sent between devices are 32-bit elements; how exact they have to be, the bound alone decides.
A program may use at most 64 MiB of HBM per device.

```python
import math
import jax
import jax.numpy as jnp
from jax import lax

PATCH = 256
TILE = 512
HALO = 64
PMAX = 3
ROWT = 8
COLT = 8
SHARDS = 8
NR = 4096
NC = 4096


def draw_positions(key, part):
    grid_shape = (ROWT, COLT, SHARDS, PMAX)
    first_key, second_key = jax.random.split(jax.random.fold_in(key, 17))
    upper_bound = TILE + HALO - PATCH
    tile_rows = jnp.arange(ROWT, dtype=jnp.int32)[:, None, None, None]
    tile_cols = jnp.arange(COLT, dtype=jnp.int32)[None, :, None, None]
    low_rows = jnp.broadcast_to(jnp.where(tile_rows == 0, 0, -HALO), grid_shape)
    high_rows = jnp.broadcast_to(jnp.where(tile_rows == ROWT - 1, TILE - PATCH, upper_bound), grid_shape)
    low_cols = jnp.broadcast_to(jnp.where(tile_cols == 0, 0, -HALO), grid_shape)
    high_cols = jnp.broadcast_to(jnp.where(tile_cols == COLT - 1, TILE - PATCH, upper_bound), grid_shape)
    row_offsets = jax.random.randint(first_key, grid_shape, low_rows, high_rows + 1, dtype=jnp.int32)
    col_offsets = jax.random.randint(second_key, grid_shape, low_cols, high_cols + 1, dtype=jnp.int32)
    row_offsets = row_offsets.at[0, 0, 0, 0].set(upper_bound).at[ROWT - 1, COLT - 1, 0, 0].set(-HALO)
    col_offsets = col_offsets.at[0, 0, 0, 0].set(upper_bound).at[ROWT - 1, COLT - 1, 0, 0].set(-HALO)
    return jnp.stack([row_offsets, col_offsets], -1)


def draw_counts(key, part):
    half_count = SHARDS // 2
    half_shape = (ROWT, COLT, half_count)
    heavy_key, side_key, middle_key = jax.random.split(jax.random.fold_in(key, 29), 3)
    heavy_pair = jax.random.randint(heavy_key, half_shape, 0, 2, dtype=jnp.int32)
    heavy_pair = heavy_pair.at[0, 0, 0].set(1)
    heavy_side = jax.random.randint(side_key, half_shape, 0, 2, dtype=jnp.int32)
    moderate = jax.random.randint(middle_key, (ROWT, COLT, SHARDS), 1, PMAX, dtype=jnp.int32)
    lower_heavy = jnp.where(heavy_side == 0, PMAX, 1)
    upper_heavy = jnp.where(heavy_side == 0, 1, PMAX)
    lower_half = jnp.where(heavy_pair == 1, lower_heavy, moderate[:, :, :half_count])
    upper_half = jnp.where(heavy_pair == 1, upper_heavy, moderate[:, :, half_count:])
    return jnp.concatenate([lower_half, upper_half], -1).astype(jnp.int32)


def shard_levels(stream_key, dims, cuts, smallest, top_value):
    factor_of = 1.0
    for dim, blocks in cuts:
        heights = jax.random.uniform(jax.random.fold_in(jax.random.fold_in(stream_key, 6), dim), (blocks,), jnp.float32, smallest / len(cuts), top_value / len(cuts))
        factor_of = factor_of * jnp.repeat(jnp.exp(heights), dims[dim] // blocks).reshape((-1,) + (1,) * (len(dims) - 1 - dim))
    return factor_of


def normal_values(key, shape, width, reach, cuts=(), held_as=jnp.bfloat16):
    result = jax.random.normal(key, shape, jnp.float32) * width
    if len(cuts) > 0:
        result = shard_levels(key, shape, cuts, -0.22, 0.18) * result
    return jnp.clip(result, min=-reach, max=reach).astype(held_as)


def setup_inputs(seed: int = 0) -> dict:
    arg_keys = jax.random.split(jax.random.key(seed), 7)
    object_field = normal_values(arg_keys[0], (2, 2, NR, NC), 0.7, 6.0, ((2, 8), (3, 8)), jnp.float32)
    probe_field = normal_values(arg_keys[1], (2, PATCH, PATCH), 0.7, 6.0, (), jnp.float32)
    prop_phase = jnp.clip(jax.random.uniform(arg_keys[2], (PATCH, PATCH), jnp.float32, -3.140625, 3.140625), -3.140625, 3.140625)
    measured = jnp.clip(jnp.exp(math.log(3.0) - 2.3025851 * jax.random.uniform(arg_keys[3], (ROWT, COLT, SHARDS, PMAX, PATCH, PATCH), jnp.float32) ** shard_levels(arg_keys[3], (ROWT, COLT, SHARDS, PMAX, PATCH, PATCH), ((0, 8), (1, 8), (2, 8)), -0.2, 0.2)), 0.3, 3.0)
    positions = draw_positions(jax.random.fold_in(arg_keys[6], 71), 0)
    counts = draw_counts(jax.random.fold_in(arg_keys[6], 71), 0)
    return {"object_field": object_field, "probe_field": probe_field, "prop_phase": prop_phase, "measured": measured, "positions": positions, "counts": counts}


def dft_tables(length):
    index_line = jnp.arange(length, dtype=jnp.int32)
    product = index_line[:, None] * index_line[None, :] % length
    angles = product.astype(jnp.float32) * (2.0 * math.pi / length)
    cosines = jnp.cos(angles) / math.sqrt(length)
    sines = jnp.sin(angles) / math.sqrt(length)
    left_fwd = jnp.stack([jnp.stack([cosines, sines], 1), jnp.stack([-sines, cosines], 1)], 0)
    right_fwd = jnp.stack([jnp.stack([cosines, -sines], 1), jnp.stack([sines, cosines], 1)], 0)
    left_inv = jnp.stack([jnp.stack([cosines, -sines], 1), jnp.stack([sines, cosines], 1)], 0)
    right_inv = jnp.stack([jnp.stack([cosines, sines], 1), jnp.stack([-sines, cosines], 1)], 0)
    return (left_fwd.astype(jnp.bfloat16), right_fwd.astype(jnp.bfloat16), left_inv.astype(jnp.bfloat16), right_inv.astype(jnp.bfloat16))

def transform(values, left_table, right_table):
    middle = jnp.einsum('qapb,pbc->qac', left_table.astype(jnp.float32), values.astype(jnp.float32), precision=lax.Precision.HIGHEST)
    middle = middle.astype(jnp.bfloat16)
    return jnp.einsum('pab,pbqc->qac', middle.astype(jnp.float32), right_table.astype(jnp.float32), precision=lax.Precision.HIGHEST)

def complex_mul(first, second):
    return jnp.stack([first[0] * second[0] - first[1] * second[1], first[0] * second[1] + first[1] * second[0]])

def conj_mul(first, second):
    return jnp.stack([first[0] * second[0] + first[1] * second[1], first[0] * second[1] - first[1] * second[0]])

def patch_grads(first_slice, second_slice, probe_field, propagator, intensity, tables):
    left_fwd, right_fwd, left_inv, right_inv = tables
    entrance = complex_mul(probe_field, first_slice).astype(jnp.bfloat16)
    spectrum = complex_mul(propagator, transform(entrance, left_fwd, right_fwd)).astype(jnp.bfloat16)
    arrived = transform(spectrum, left_inv, right_inv)
    leaving = complex_mul(second_slice, arrived).astype(jnp.bfloat16)
    far_field = transform(leaving, left_fwd, right_fwd)
    power = far_field[0] * far_field[0] + far_field[1] * far_field[1]
    residual = ((power - intensity)[None] * far_field).astype(jnp.bfloat16)
    back_second = transform(residual, left_inv, right_inv)
    grad_second = conj_mul(arrived, back_second)
    through = conj_mul(second_slice, back_second).astype(jnp.bfloat16)
    back_spectrum = conj_mul(propagator, transform(through, left_fwd, right_fwd)).astype(jnp.bfloat16)
    back_first = transform(back_spectrum, left_inv, right_inv)
    grad_first = conj_mul(probe_field, back_first)
    return jnp.stack([grad_first, grad_second])

def reference(object_field, probe_field, prop_phase, measured, positions, counts):
    tables = dft_tables(PATCH)
    propagator = jnp.stack([jnp.cos(prop_phase), jnp.sin(prop_phase)])
    padded = jnp.pad(object_field, ((0, 0), (0, 0), (HALO, HALO), (HALO, HALO)))
    gradient = jnp.zeros(padded.shape, jnp.float32)
    tile_rows, tile_cols, shard_count = counts.shape
    grid_shape = (tile_rows, tile_cols, shard_count, PMAX)
    row_index = jnp.broadcast_to(jnp.arange(tile_rows, dtype=jnp.int32)[:, None, None, None], grid_shape).reshape(-1)
    col_index = jnp.broadcast_to(jnp.arange(tile_cols, dtype=jnp.int32)[None, :, None, None], grid_shape).reshape(-1)
    slot_index = jnp.broadcast_to(jnp.arange(PMAX, dtype=jnp.int32)[None, None, None, :], grid_shape)
    live_slot = (slot_index < counts[..., None]).reshape(-1)
    corners = positions.reshape(-1, 2).astype(jnp.int32)
    intensities = measured.reshape(-1, PATCH, PATCH)
    zero_index = jnp.zeros((), jnp.int32)

    def scan_step(carry, item):
        tile_row, tile_col, corner, on_flag, intensity = item
        row_start = (tile_row * TILE + corner[0] + HALO).astype(jnp.int32)
        col_start = (tile_col * TILE + corner[1] + HALO).astype(jnp.int32)
        starts = (zero_index, zero_index, row_start, col_start)

        def one_patch(current):
            window = lax.dynamic_slice(padded, starts, (2, 2, PATCH, PATCH))
            update = patch_grads(window[0], window[1], probe_field, propagator, intensity, tables)
            present = lax.dynamic_slice(current, starts, (2, 2, PATCH, PATCH))
            return lax.dynamic_update_slice(current, present + update, starts)

        def unchanged(current):
            return current
        return (lax.cond(on_flag, one_patch, unchanged, carry), None)
    gradient, _ = lax.scan(scan_step, gradient, (row_index, col_index, corners, live_slot, intensities))
    return gradient[:, :, HALO:-HALO, HALO:-HALO]
```

```python
import functools
import math

import jax
import jax.numpy as jnp
import numpy as np
from jax import lax
from jax.experimental import pallas as pl
from jax.experimental.pallas import tpu as pltpu
from jax.sharding import PartitionSpec as P

PATCH = 256
HALO = 64
PMAX = 3
LANE = 128
BLOCK = 64
PIECE = 8
FAR = 4
CHAINS = ((1, 0, 3), (1, 1, 4), (-1, 0, 4), (-1, 1, 3))
MESH = pl.DeviceIdType.MESH


def halo_kernel(sizes, field_ref, phase_ref, probe_ref, half_ref, measured_ref, ext_ref, prop_ref, probe_out, measured_out,
                fwd_ref, inv_ref, halves, load_sem, core_sem, row_send, row_recv, ring_send, ring_recv,
                side_send, side_recv, corner_send, corner_recv):
    rows, cols, depth = sizes
    r, c, z = (lax.axis_index(name) for name in ("row", "col", "scan"))
    has_left, has_right = c > 0, c < cols - 1
    has_up, has_down = r > 0, r < rows - 1
    around = lambda step: lax.rem(z + (step + depth), depth)
    core = field_ref.shape[1]
    barrier = pltpu.get_barrier_semaphore()

    def greet(device):
        pl.semaphore_signal(barrier, inc=1, device_id=device, device_id_type=MESH)

    for step in (1, -1):
        greet((r, c, around(step)))
    pl.when(has_left)(lambda: greet((r, c - 1, z)))
    pl.when(has_right)(lambda: greet((r, c + 1, z)))
    pl.when(has_up)(lambda: greet((r - 1, c, z)))
    pl.when(has_down)(lambda: greet((r + 1, c, z)))

    fills = [
        pltpu.make_async_copy(
            field_ref.at[:, :, t * LANE : (t + 1) * LANE], ext_ref.at[:, t + 1, HALO : HALO + core, :], core_sem.at[t])
        for t in range(4)
    ]
    for fill in fills:
        fill.start()
    loads = [
        pltpu.make_async_copy(source, target, load_sem.at[i])
        for i, (source, target) in enumerate((
            (phase_ref, prop_ref.at[0]), (half_ref, halves), (probe_ref, probe_out), (measured_ref, measured_out)))
    ]
    for load in loads:
        load.start()
    for fill in fills:
        fill.wait()

    count = jnp.int32(2)
    for flag in (has_left, has_right, has_up, has_down):
        count = count + flag.astype(jnp.int32)
    pl.semaphore_wait(barrier, count)

    def piece_rows(first, piece):
        return pl.ds(pl.multiple_of(first + piece * PIECE, PIECE), PIECE)

    starts = (0, HALO + core)

    def row_copy(side):
        source = piece_rows(core if side == 0 else HALO, z)
        return pltpu.make_async_remote_copy(
            src_ref=ext_ref.at[:, 1:5, source, :], dst_ref=ext_ref.at[:, 1:5, piece_rows(starts[side], z), :],
            send_sem=row_send.at[side], recv_sem=row_recv.at[side],
            device_id=(r + 1 - 2 * side, c, z), device_id_type=MESH)

    pl.when(has_down)(lambda: row_copy(0).start())
    pl.when(has_up)(lambda: row_copy(1).start())

    def side_copy(side):
        tile, target = ((4, 0), (1, 5))[side]
        return pltpu.make_async_remote_copy(
            src_ref=ext_ref.at[:, tile, HALO : HALO + core, :], dst_ref=ext_ref.at[:, target, HALO : HALO + core, :],
            send_sem=side_send.at[side], recv_sem=side_recv.at[side],
            device_id=(r, c + 1 - 2 * side, z), device_id_type=MESH)

    pl.when(has_right)(lambda: side_copy(0).start())
    pl.when(has_left)(lambda: side_copy(1).start())

    def ring_copy(side, chain, step):
        direction, part, _ = CHAINS[chain]
        place = ext_ref.at[:, 2 * part + 1 : 2 * part + 3, piece_rows(starts[side], around(-direction * step)), :]
        return pltpu.make_async_remote_copy(
            src_ref=place, dst_ref=place,
            send_sem=ring_send.at[side, chain, step], recv_sem=ring_recv.at[side, chain, step],
            device_id=(r, c, around(direction)), device_id_type=MESH)

    def corner_copy(side, part, piece, slot):
        tile, target = ((1, 5), (4, 0))[part]
        place = piece_rows(starts[side], piece)
        return pltpu.make_async_remote_copy(
            src_ref=ext_ref.at[:, tile, place, :], dst_ref=ext_ref.at[:, target, place, :],
            send_sem=corner_send.at[side, part, slot], recv_sem=corner_recv.at[side, part, slot],
            device_id=(r, c + 2 * part - 1, z), device_id_type=MESH)

    faces = ((has_left, has_right), (has_right, has_left))
    live = (has_up, has_down)
    corners = []

    def send_corner(side, part, offset):
        slot = len([1 for entry in corners if entry[:2] == (side, part)])
        corners.append((side, part, offset, slot))
        pl.when(faces[part][0])(lambda: corner_copy(side, part, around(offset), slot).start())

    loads[0].wait()
    phase = prop_ref[0]
    prop_ref[0] = jnp.cos(phase)
    prop_ref[1] = jnp.sin(phase)
    loads[1].wait()
    cosines, sines = halves[0], halves[1]
    for ref, above, below in ((fwd_ref, sines, -sines), (inv_ref, -sines, sines)):
        ref[:PATCH, :PATCH] = cosines
        ref[PATCH:, PATCH:] = cosines
        ref[:PATCH, PATCH:] = above
        ref[PATCH:, :PATCH] = below

    for step in range(FAR + 1):
        for side in range(2):
            @pl.when(live[side])
            def _():
                if step == 0:
                    row_copy(side).wait_recv()
                    for part in range(2):
                        send_corner(side, part, 0)
                for chain, (direction, part, length) in enumerate(CHAINS):
                    if 0 < step <= length:
                        ring_copy(side, chain, step - 1).wait_recv()
                    if step < length:
                        ring_copy(side, chain, step).start()
                    if 0 < step <= length:
                        send_corner(side, part, -direction * step)

    for side in range(2):
        pl.when((has_left, has_right)[side])(lambda: side_copy(side).wait_recv())
        @pl.when(live[side])
        def _():
            for entry_side, part, offset, slot in corners:
                if entry_side == side:
                    pl.when(faces[part][1])(lambda: corner_copy(side, part, around(offset), slot).wait_recv())
                    pl.when(faces[part][0])(lambda: corner_copy(side, part, around(offset), slot).wait_send())
            for chain, (_, _, length) in enumerate(CHAINS):
                for step in range(length):
                    ring_copy(side, chain, step).wait_send()
    for load in loads[2:]:
        load.wait()
    pl.when(has_down)(lambda: row_copy(0).wait_send())
    pl.when(has_up)(lambda: row_copy(1).wait_send())
    pl.when(has_right)(lambda: side_copy(0).wait_send())
    pl.when(has_left)(lambda: side_copy(1).wait_send())

def halo_call(sizes, field, phase, probe, halves, measured):
    planes, core, _ = field.shape
    dma = pltpu.SemaphoreType.DMA
    depth = sizes[2]
    vmem = pl.BlockSpec(memory_space=pltpu.VMEM)
    return pl.pallas_call(
        functools.partial(halo_kernel, sizes),
        out_shape=(
            jax.ShapeDtypeStruct((planes, 6, core + 2 * HALO, LANE), jnp.float32),
            jax.ShapeDtypeStruct((2, PATCH, PATCH), jnp.float32),
            jax.ShapeDtypeStruct(probe.shape, jnp.float32),
            jax.ShapeDtypeStruct(measured.shape, jnp.float32),
            jax.ShapeDtypeStruct((2 * PATCH, 2 * PATCH), jnp.bfloat16),
            jax.ShapeDtypeStruct((2 * PATCH, 2 * PATCH), jnp.bfloat16),
        ),
        in_specs=[pl.BlockSpec(memory_space=pltpu.HBM)] * 5,
        out_specs=(vmem,) * 6,
        scratch_shapes=[
            pltpu.VMEM((2, PATCH, PATCH), jnp.bfloat16), dma((4,)),
            dma((4,)), dma((2,)), dma((2,)), dma((2, 4, FAR)), dma((2, 4, FAR)),
            dma((2,)), dma((2,)), dma((2, 2, depth)), dma((2, 2, depth)),
        ],
        compiler_params=pltpu.CompilerParams(collective_id=0, has_side_effects=True, vmem_limit_bytes=24 << 20),
    )(field, phase, probe, halves, measured)


def dft_halves():
    k = np.arange(PATCH)
    ang = ((k[:,None]*k[None,:])%PATCH).astype(np.float32)*np.float32(2.0*math.pi/PATCH)
    scale = np.float32(math.sqrt(PATCH))
    return np.stack([np.cos(ang)/scale, np.sin(ang)/scale]).astype(jnp.bfloat16)

def transform(real, imag, left, right):
    rows = jnp.concatenate([real, imag], 0)
    middle = jnp.dot(left, rows, preferred_element_type=jnp.float32).astype(jnp.bfloat16)
    middle = jnp.concatenate([middle[:PATCH], middle[PATCH:]], 1)
    out = jnp.dot(middle, right, preferred_element_type=jnp.float32)
    return out[:, :PATCH], out[:, PATCH:]

def patch_kernel(count_ref, corner_ref, object_ref, prop_ref, probe_ref, measured_ref, fwd_ref, inv_ref, grad_ref):
    grad_ref[...] = jnp.zeros_like(grad_ref)
    bf = lambda x: x.astype(jnp.bfloat16)

    def slot(k, carry):
        row = corner_ref[0, k] + HALO
        col = corner_ref[1, k] + LANE
        tile = col // LANE
        shift = col - tile * LANE
        back = lax.rem(LANE - shift, LANE)
        lanes = lax.broadcasted_iota(jnp.int32, (PATCH, LANE), 1)
        early, late = lanes < LANE - shift, lanes < shift
        def window(plane):
            turned = [pltpu.roll(object_ref[plane, tile + t, pl.ds(row, PATCH), :], back, 1) for t in range(3)]
            return jnp.concatenate([jnp.where(early, turned[0], turned[1]), jnp.where(early, turned[1], turned[2])], 1)
        def place(plane, value):
            first, second = (pltpu.roll(value[:, t*LANE:(t+1)*LANE], shift, 1) for t in range(2))
            zero = jnp.zeros_like(first)
            for t, part in enumerate((jnp.where(late, zero, first), jnp.where(late, first, second), jnp.where(late, second, zero))):
                grad_ref[plane, tile + t, pl.ds(row, PATCH), :] += part
        pr, pi = probe_ref[0], probe_ref[1]
        hr, hi = prop_ref[0], prop_ref[1]
        fwd, inv = fwd_ref, inv_ref
        ar, ai = window(0), window(1)
        sr, si = transform(bf(pr*ar-pi*ai), bf(pr*ai+pi*ar), fwd[...], inv[...])
        wr, wi = transform(bf(hr*sr-hi*si), bf(hr*si+hi*sr), inv[...], fwd[...])
        br, bi = window(2), window(3)
        fr, fi = transform(bf(br*wr-bi*wi), bf(br*wi+bi*wr), fwd[...], inv[...])
        level = fr*fr + fi*fi - measured_ref[k]
        gr, gi = transform(bf(level*fr), bf(level*fi), inv[...], fwd[...])
        place(2, wr*gr+wi*gi)
        place(3, wr*gi-wi*gr)
        tr, ti = transform(bf(br*gr+bi*gi), bf(br*gi-bi*gr), fwd[...], inv[...])
        qr, qi = transform(bf(hr*tr+hi*ti), bf(hr*ti-hi*tr), inv[...], fwd[...])
        place(0, pr*qr+pi*qi)
        place(1, pr*qi-pi*qr)
        return carry
    lax.fori_loop(0, count_ref[0], slot, 0)

def patch_call(count, corners, ext, *rest):
    v = pl.BlockSpec(memory_space=pltpu.VMEM); s = pl.BlockSpec(memory_space=pltpu.SMEM)
    return pl.pallas_call(patch_kernel,
        out_shape=jax.ShapeDtypeStruct(ext.shape, jnp.float32),
        in_specs=[s, s] + [v] * 6, out_specs=v,
        compiler_params=pltpu.CompilerParams(vmem_limit_bytes=24<<20),
    )(count, corners, ext, *rest)


def reduce_kernel(sizes, grad_ref, out_ref, pack, took, stage, rim, rim_slot, slot, rim_sum, far,
                  fold_send, fold_recv, rim_send, rim_recv, main_send, main_recv, far_send, far_recv):
    rows, cols, depth = sizes
    r, c, z = (lax.axis_index(name) for name in ("row", "col", "scan"))
    last = depth - 1
    has_left, has_right = c > 0, c < cols - 1
    has_up, has_down = r > 0, r < rows - 1
    takes_top = jnp.logical_and(z == last, has_down)
    takes_bottom = jnp.logical_and(z == 0, has_up)
    around = lambda step: lax.rem(z + (step + depth), depth)
    barrier = pltpu.get_barrier_semaphore()

    def greet(device):
        pl.semaphore_signal(barrier, inc=1, device_id=device, device_id_type=MESH)

    for step in (1, -1):
        greet((r, c, around(step)))
    pl.when(has_left)(lambda: greet((r, c - 1, z)))
    pl.when(has_right)(lambda: greet((r, c + 1, z)))

    @pl.when(takes_top)
    def _():
        for other in range(depth):
            greet((r + 1, c, other))

    @pl.when(takes_bottom)
    def _():
        for other in range(depth):
            greet((r - 1, c, other))

    blocks = grad_ref.shape[2] // BLOCK
    half = BLOCK // 2
    for side, tile in ((0, 0), (1, 5)):
        for b in range(blocks):
            top = grad_ref[:, tile, b * BLOCK : b * BLOCK + half, :]
            low = grad_ref[:, tile, b * BLOCK + half : (b + 1) * BLOCK, :]
            pack[side, b] = top + pltpu.roll(low, BLOCK, 2)

    count = jnp.int32(2)
    for flag in (has_left, has_right, has_up, has_down):
        count = count + flag.astype(jnp.int32)
    pl.semaphore_wait(barrier, count)

    def fold_copy(side, block):
        return pltpu.make_async_remote_copy(
            src_ref=pack.at[side, block], dst_ref=took.at[side, block],
            send_sem=fold_send.at[side, block], recv_sem=fold_recv.at[side, block],
            device_id=(r, c + (2 * side - 1), z), device_id_type=MESH)

    steps = (4, 3, -3, 2, -2, 1, -1, 0)
    order = [0, blocks - 1] + [around(step) + 1 for step in steps]

    @pl.when(has_left)
    def _():
        for b in order:
            fold_copy(0, b).start()

    @pl.when(has_right)
    def _():
        for b in order:
            fold_copy(1, b).start()

    @pl.when(jnp.logical_not(has_right))
    def _():
        took[0] = jnp.zeros_like(took[0])

    @pl.when(jnp.logical_not(has_left))
    def _():
        took[1] = jnp.zeros_like(took[1])

    def await_fold(block):
        pl.when(has_right)(lambda: fold_copy(0, block).wait_recv())
        pl.when(has_left)(lambda: fold_copy(1, block).wait_recv())

    right_lanes = lax.broadcasted_iota(jnp.int32, (half, LANE), 1) >= BLOCK

    def local(block, plane, part):
        start = pl.multiple_of(block * BLOCK, BLOCK)
        tiles = [grad_ref[plane, 2 * part + 1 + t, pl.ds(start, BLOCK), :] for t in range(2)]
        side, edge = (1, 0) if part == 0 else (0, 1)
        packed = took[side, block, plane]
        turned = pltpu.roll(packed, BLOCK, 1)
        zero = jnp.zeros_like(packed)
        if part == 0:
            pieces = [jnp.where(right_lanes, zero, packed), jnp.where(right_lanes, zero, turned)]
        else:
            pieces = [jnp.where(right_lanes, packed, zero), jnp.where(right_lanes, turned, zero)]
        tiles[edge] = tiles[edge] + jnp.concatenate(pieces, 0)
        return tiles

    for index, block in enumerate((0, blocks - 1)):
        await_fold(block)
        for part in range(2):
            for plane in range(4):
                for t, tile in enumerate(local(block, plane, part)):
                    rim[part, index, plane, t] = tile

    def rim_copy(chain, step, source):
        direction = CHAINS[chain][0]
        return pltpu.make_async_remote_copy(
            src_ref=source, dst_ref=rim_slot.at[chain, step],
            send_sem=rim_send.at[chain, step], recv_sem=rim_recv.at[chain, step],
            device_id=(r, c, around(direction)), device_id_type=MESH)

    def main_copy(chain, step, sub, source):
        direction = CHAINS[chain][0]
        return pltpu.make_async_remote_copy(
            src_ref=source, dst_ref=slot.at[chain, step, sub],
            send_sem=main_send.at[chain, step, sub], recv_sem=main_recv.at[chain, step, sub],
            device_id=(r, c, around(direction)), device_id_type=MESH)

    def rim_rows(piece):
        return pl.ds(pl.multiple_of(piece * PIECE, PIECE), PIECE)

    sent = []

    def rim_round(k):
        for chain, (direction, part, length) in enumerate(CHAINS):
            step = k - (FAR - length)
            if step < 0:
                continue
            piece = rim_rows(around(direction * (FAR - k)))
            if step == 0:
                source = rim.at[part, :, :, :, piece, :]
            else:
                source = rim_slot.at[chain, step - 1]
                rim_copy(chain, step - 1, source).wait_recv()
                source[...] += rim[part, :, :, :, piece, :]
            copy = rim_copy(chain, step, source)
            copy.start()
            sent.append(copy)

    def main_round(k, sub):
        for chain, (direction, part, length) in enumerate(CHAINS):
            step = k - (FAR - length)
            if step < 0:
                continue
            block = around(direction * (FAR - k)) + 1
            if step == 0:
                source = stage.at[chain, sub]
            else:
                source = slot.at[chain, step - 1, sub]
                main_copy(chain, step - 1, sub, source).wait_recv()
            for p in range(2):
                for t, tile in enumerate(local(block, 2 * sub + p, part)):
                    if step == 0:
                        source[p, t] = tile
                    else:
                        source[p, t] += tile
            copy = main_copy(chain, step, sub, source)
            copy.start()
            sent.append(copy)

    def await_round(k):
        for step in ((4,), (3, -3), (2, -2), (1, -1), (0,))[k]:
            await_fold(around(step) + 1)

    rim_round(0)
    await_round(0)
    main_round(0, 0)
    rim_round(1)
    main_round(0, 1)
    rim_round(2)
    await_round(1)
    main_round(1, 0)
    rim_round(3)
    main_round(1, 1)
    own = rim_rows(z)
    for chain, (direction, part, length) in enumerate(CHAINS):
        rim_copy(chain, length - 1, rim_slot.at[chain, length - 1]).wait_recv()
    for part in range(2):
        ahead, behind = [(i, n) for i, (_, q, n) in enumerate(CHAINS) if q == part]
        total = rim[part, :, :, :, own, :] + rim_slot[ahead[0], ahead[1] - 1] + rim_slot[behind[0], behind[1] - 1]
        rim_sum[:, :, 2 * part : 2 * part + 2] = total

    def far_copy(side):
        target = (r - 1, c, last) if side == 0 else (r + 1, c, 0)
        return pltpu.make_async_remote_copy(
            src_ref=rim_sum.at[side], dst_ref=far.at[:, :, own, :],
            send_sem=far_send.at[side], recv_sem=far_recv.at[z],
            device_id=target, device_id_type=MESH)

    pl.when(has_up)(lambda: far_copy(0).start())
    pl.when(has_down)(lambda: far_copy(1).start())
    await_round(2)
    main_round(2, 0)
    main_round(2, 1)
    await_round(3)
    main_round(3, 0)
    main_round(3, 1)
    await_round(4)

    for sub in range(2):
        for chain, (direction, part, length) in enumerate(CHAINS):
            main_copy(chain, length - 1, sub, slot.at[chain, length - 1, sub]).wait_recv()
        for part in range(2):
            ahead, behind = [(i, n) for i, (_, q, n) in enumerate(CHAINS) if q == part]
            for p in range(2):
                tiles = local(z + 1, 2 * sub + p, part)
                for t in range(2):
                    out_ref[2 * sub + p, :, (2 * part + t) * LANE : (2 * part + t + 1) * LANE] = (
                        tiles[t] + slot[ahead[0], ahead[1] - 1, sub, p, t] + slot[behind[0], behind[1] - 1, sub, p, t])

    @pl.when(jnp.logical_or(takes_top, takes_bottom))
    def _():
        for other in range(depth):
            pltpu.make_async_remote_copy(
                src_ref=rim_sum.at[0], dst_ref=far.at[:, :, other * PIECE : (other + 1) * PIECE, :],
                send_sem=far_send.at[0], recv_sem=far_recv.at[other],
                device_id=(r, c, around(1)), device_id_type=MESH).wait_recv()
        for plane in range(4):
            for t in range(4):
                out_ref[plane, :, t * LANE : (t + 1) * LANE] += far[plane, t]

    for copy in sent:
        copy.wait_send()
    pl.when(has_up)(lambda: far_copy(0).wait_send())
    pl.when(has_down)(lambda: far_copy(1).wait_send())

    @pl.when(has_left)
    def _():
        for b in range(blocks):
            fold_copy(0, b).wait_send()

    @pl.when(has_right)
    def _():
        for b in range(blocks):
            fold_copy(1, b).wait_send()

def reduce_call(sizes, grad):
    blocks = grad.shape[2] // BLOCK
    f32 = jnp.float32
    dma = pltpu.SemaphoreType.DMA
    return pl.pallas_call(
        functools.partial(reduce_kernel, sizes),
        out_shape=jax.ShapeDtypeStruct((4, BLOCK, 4 * LANE), f32),
        in_specs=[pl.BlockSpec(memory_space=pltpu.VMEM)],
        out_specs=pl.BlockSpec(memory_space=pltpu.VMEM),
        scratch_shapes=[
            pltpu.VMEM((2, blocks, 4, BLOCK // 2, LANE), f32),
            pltpu.VMEM((2, blocks, 4, BLOCK // 2, LANE), f32),
            pltpu.VMEM((4, 2, 2, 2, BLOCK, LANE), f32),
            pltpu.VMEM((2, 2, 4, 2, BLOCK, LANE), f32),
            pltpu.VMEM((4, FAR, 2, 4, 2, PIECE, LANE), f32),
            pltpu.VMEM((4, FAR, 2, 2, 2, BLOCK, LANE), f32),
            pltpu.VMEM((2, 4, 4, PIECE, LANE), f32),
            pltpu.VMEM((4, 4, BLOCK, LANE), f32),
            dma((2, blocks)), dma((2, blocks)),
            dma((4, FAR)), dma((4, FAR)),
            dma((4, FAR, 2)), dma((4, FAR, 2)),
            dma((2,)), dma((sizes[2],)),
        ],
        compiler_params=pltpu.CompilerParams(collective_id=1, has_side_effects=True, vmem_limit_bytes=32 << 20),
    )(grad)


def shards(sizes, object_field, probe_field, prop_phase, measured, positions, counts):
    loaded = halo_call(
        sizes,
        object_field.reshape(4, *object_field.shape[2:]),
        prop_phase,
        probe_field,
        jnp.asarray(dft_halves()),
        measured.reshape(PMAX, PATCH, PATCH),
    )
    gradient = patch_call(counts.reshape(1), positions.reshape(PMAX, 2).T, *loaded)
    return reduce_call(sizes, gradient).reshape(2, 2, BLOCK, 4 * LANE)


def solution(mesh):
    placed = (
        P(None, None, "row", "col"),
        P(),
        P(),
        P("row", "col", "scan", None, None, None),
        P("row", "col", "scan", None, None),
        P("row", "col", "scan"),
    )
    sizes = tuple(mesh.shape[name] for name in ("row", "col", "scan"))
    return jax.shard_map(
        functools.partial(shards, sizes),
        mesh=mesh,
        in_specs=placed,
        out_specs=P(None, None, ("row", "scan"), "col"),
        check_vma=False,
    )
```

```python
import functools
import math

import jax
import jax.numpy as jnp
import numpy as np
from jax import lax
from jax.experimental import pallas as pl
from jax.experimental.pallas import tpu as pltpu
from jax.sharding import PartitionSpec as P

PATCH = 256
HALO = 64
PMAX = 3
LANE = 128
BLOCK = 64
PIECE = 8
FAR = 4
CHAINS = ((1, 0, 3), (1, 1, 4), (-1, 0, 4), (-1, 1, 3))
MESH = pl.DeviceIdType.MESH


def dft_halves():
    k = np.arange(PATCH)
    angles = ((k[:, None] * k[None, :]) % PATCH).astype(np.float32) * np.float32(2.0 * math.pi / PATCH)
    scale = np.float32(math.sqrt(PATCH))
    return np.stack([np.cos(angles) / scale, np.sin(angles) / scale]).astype(jnp.bfloat16)


def stacked(real, imag):
    return jnp.concatenate([real.astype(jnp.bfloat16), imag.astype(jnp.bfloat16)], 0)


def transform(rows, left, right):
    middle = jnp.dot(left, rows, preferred_element_type=jnp.float32).astype(jnp.bfloat16)
    middle = jnp.concatenate([middle[:PATCH], middle[PATCH:]], 1)
    out = jnp.dot(middle, right, preferred_element_type=jnp.float32)
    return out[:, :PATCH], out[:, PATCH:]


def fused_kernel(
    sizes, count_ref, corner_ref, field_ref, phase_ref, probe_hbm, half_ref, measured_hbm, out_ref,
    ext_ref, prop_ref, probe_ref, measured_ref, fwd_ref, inv_ref, halves, through, placed,
    pack, took, stage, rim, rim_slot, slot, rim_sum, far,
    load_sem, core_sem, row_send, row_recv, ring_send, ring_recv, side_send, side_recv, corner_send, corner_recv,
    fold_send, fold_recv, rim_send, rim_recv, main_send, main_recv, far_send, far_recv,
):
    rows, cols, depth = sizes
    r, c, z = (lax.axis_index(name) for name in ("row", "col", "scan"))
    last = depth - 1
    has_left, has_right = c > 0, c < cols - 1
    has_up, has_down = r > 0, r < rows - 1
    core = field_ref.shape[1]
    blocks = ext_ref.shape[2] // BLOCK
    half = BLOCK // 2

    def around(step):
        return lax.rem(z + (step + depth), depth)

    def remote(source, target, send, recv, device):
        return pltpu.make_async_remote_copy(
            src_ref=source, dst_ref=target, send_sem=send, recv_sem=recv, device_id=device, device_id_type=MESH
        )

    barrier = pltpu.get_barrier_semaphore()

    def greet(device):
        pl.semaphore_signal(barrier, inc=1, device_id=device, device_id_type=MESH)

    pl.when(has_up)(lambda: greet((r - 1, c, z)))
    pl.when(has_down)(lambda: greet((r + 1, c, z)))
    pl.when(has_left)(lambda: greet((r, c - 1, z)))
    pl.when(has_right)(lambda: greet((r, c + 1, z)))
    for step in (1, -1):
        greet((r, c, around(step)))

    fills = [
        pltpu.make_async_copy(
            field_ref.at[:, :, t * LANE : (t + 1) * LANE], ext_ref.at[:, t + 1, HALO : HALO + core, :], core_sem.at[t]
        )
        for t in range(4)
    ]
    for fill in fills:
        fill.start()
    pairs = ((phase_ref, prop_ref.at[0]), (half_ref, halves), (probe_hbm, probe_ref), (measured_hbm, measured_ref))
    loads = [pltpu.make_async_copy(source, target, load_sem.at[i]) for i, (source, target) in enumerate(pairs)]
    for load in loads:
        load.start()
    for fill in fills:
        fill.wait()
    count = jnp.int32(2)
    for flag in (has_left, has_right, has_up, has_down):
        count = count + flag.astype(jnp.int32)
    pl.semaphore_wait(barrier, count)

    def piece_rows(first, piece):
        return pl.ds(pl.multiple_of(first + piece * PIECE, PIECE), PIECE)

    starts = (0, HALO + core)

    def row_copy(side):
        source = piece_rows(core if side == 0 else HALO, z)
        return remote(
            ext_ref.at[:, 1:5, source, :], ext_ref.at[:, 1:5, piece_rows(starts[side], z), :],
            row_send.at[side], row_recv.at[side], (r + 1 - 2 * side, c, z),
        )

    def side_copy(side):
        tile, target = ((4, 0), (1, 5))[side]
        return remote(
            ext_ref.at[:, tile, HALO : HALO + core, :], ext_ref.at[:, target, HALO : HALO + core, :],
            side_send.at[side], side_recv.at[side], (r, c + 1 - 2 * side, z),
        )

    def ring_copy(side, chain, step):
        direction, part, _ = CHAINS[chain]
        place = ext_ref.at[:, 2 * part + 1 : 2 * part + 3, piece_rows(starts[side], around(-direction * step)), :]
        return remote(
            place, place, ring_send.at[side, chain, step], ring_recv.at[side, chain, step], (r, c, around(direction))
        )

    def corner_copy(side, part, offset, index):
        tile, target = ((1, 5), (4, 0))[part]
        place = piece_rows(starts[side], around(offset))
        return remote(
            ext_ref.at[:, tile, place, :], ext_ref.at[:, target, place, :],
            corner_send.at[side, part, index], corner_recv.at[side, part, index], (r, c + 2 * part - 1, z),
        )

    pl.when(has_down)(lambda: row_copy(0).start())
    pl.when(has_up)(lambda: row_copy(1).start())

    loads[0].wait()
    phase = prop_ref[0]
    prop_ref[0] = jnp.cos(phase)
    prop_ref[1] = jnp.sin(phase)
    loads[1].wait()
    cosines, sines = halves[0], halves[1]
    for ref, above, below in ((fwd_ref, sines, -sines), (inv_ref, -sines, sines)):
        ref[:PATCH, :PATCH] = cosines
        ref[PATCH:, PATCH:] = cosines
        ref[:PATCH, PATCH:] = above
        ref[PATCH:, :PATCH] = below

    targets = ((has_left, has_right), (has_right, has_left))
    live = (has_up, has_down)
    corners = []

    def send_corner(side, part, offset):
        index = len([1 for entry in corners if entry[:2] == (side, part)])
        corners.append((side, part, offset, index))
        pl.when(targets[part][0])(lambda: corner_copy(side, part, offset, index).start())

    for step in range(FAR + 1):
        for side in range(2):

            @pl.when(live[side])
            def _():
                if step == 0:
                    row_copy(side).wait_recv()
                for chain, (direction, part, length) in enumerate(CHAINS):
                    if 0 < step <= length:
                        ring_copy(side, chain, step - 1).wait_recv()
                    if step < length:
                        ring_copy(side, chain, step).start()
                for chain, (direction, part, length) in enumerate(CHAINS):
                    if step == 0 and chain < 2:
                        send_corner(side, chain, 0)
                    if 0 < step <= length:
                        send_corner(side, part, -direction * step)

        if step == 0:
            pl.when(has_right)(lambda: side_copy(0).start())
            pl.when(has_left)(lambda: side_copy(1).start())
            placed[...] = jnp.zeros_like(placed)

    for side in range(2):
        pl.when((has_left, has_right)[side])(lambda: side_copy(side).wait_recv())

        @pl.when(live[side])
        def _():
            for at, part, offset, index in corners:
                if at == side:
                    pl.when(targets[part][1])(lambda: corner_copy(side, part, offset, index).wait_recv())

    for load in loads[2:]:
        load.wait()

    def position(k):
        row = jnp.clip(corner_ref[0, k], -HALO, core + HALO - PATCH) + HALO
        col = jnp.clip(corner_ref[1, k], -HALO, core + HALO - PATCH) + LANE
        tile = lax.shift_right_logical(col, 7)
        return row, tile, col - tile * LANE

    patches = count_ref[0]
    lanes = lax.broadcasted_iota(jnp.int32, (PATCH, LANE), 1)

    def place(k, plane, value, shift):
        late = lanes < shift
        first, second = (pltpu.roll(value[:, t * LANE : (t + 1) * LANE], shift, 1) for t in range(2))
        zero = jnp.zeros_like(first)
        parts = (jnp.where(late, zero, first), jnp.where(late, first, second), jnp.where(late, second, zero))
        for t, tile in enumerate(parts):
            placed[k, plane, t + 1, BLOCK : BLOCK + PATCH, :] = jnp.where(k < patches, tile, 0.0)

    def outward(k, carry):
        row, tile, shift = position(k)
        back = lax.rem(LANE - shift, LANE)
        early = lanes < LANE - shift

        def window(plane):
            turned = [pltpu.roll(ext_ref[plane, tile + t, pl.ds(row, PATCH), :], back, 1) for t in range(3)]
            return jnp.concatenate(
                [jnp.where(early, turned[0], turned[1]), jnp.where(early, turned[1], turned[2])], 1
            )

        pr, pi = probe_ref[0], probe_ref[1]
        hr, hi = prop_ref[0], prop_ref[1]
        ar, ai = window(0), window(1)
        sr, si = transform(stacked(pr * ar - pi * ai, pr * ai + pi * ar), fwd_ref[...], inv_ref[...])
        wr, wi = transform(stacked(hr * sr - hi * si, hr * si + hi * sr), inv_ref[...], fwd_ref[...])
        br, bi = window(2), window(3)
        fr, fi = transform(stacked(br * wr - bi * wi, br * wi + bi * wr), fwd_ref[...], inv_ref[...])
        level = fr * fr + fi * fi - measured_ref[k]
        gr, gi = transform(stacked(level * fr, level * fi), inv_ref[...], fwd_ref[...])
        place(k, 2, wr * gr + wi * gi, shift)
        place(k, 3, wr * gi - wi * gr, shift)
        through[k] = stacked(br * gr + bi * gi, br * gi - bi * gr)
        return carry

    def inward(k, carry):
        _, _, shift = position(k)
        pr, pi = probe_ref[0], probe_ref[1]
        hr, hi = prop_ref[0], prop_ref[1]
        tr, ti = transform(through[k], fwd_ref[...], inv_ref[...])
        qr, qi = transform(stacked(hr * tr + hi * ti, hr * ti - hi * tr), inv_ref[...], fwd_ref[...])
        place(k, 0, pr * qr + pi * qi, shift)
        place(k, 1, pr * qi - pi * qr, shift)
        return carry

    spots = [position(k)[:2] for k in range(PMAX)]

    def gathered(plane, tile, block):
        total = None
        for k, (row, first) in enumerate(spots):
            at = jnp.clip(block * BLOCK - row, -BLOCK, PATCH) + BLOCK
            value = placed[k, plane, jnp.clip(tile - first, -1, 3) + 1, pl.ds(at, BLOCK), :]
            total = value if total is None else total + value
        return total

    def fold_copy(side, slab, block):
        return remote(
            pack.at[side, slab, block], took.at[side, slab, block],
            fold_send.at[side, slab, block], fold_recv.at[side, slab, block], (r, c + (2 * side - 1), z),
        )

    def fold(slab):
        steps = (4, 3, -3, 2, -2, 1, -1, 0)
        for block in [0, blocks - 1] + [around(step) + 1 for step in steps]:
            for side, tile in ((0, 0), (1, 5)):
                for p in range(2):
                    whole = gathered(2 * slab + p, tile, block)
                    pack[side, slab, block, p] = whole[:half] + pltpu.roll(whole[half:], BLOCK, 1)
            pl.when(has_left)(lambda: fold_copy(0, slab, block).start())
            pl.when(has_right)(lambda: fold_copy(1, slab, block).start())

    def await_fold(slab, block):
        pl.when(has_right)(lambda: fold_copy(0, slab, block).wait_recv())
        pl.when(has_left)(lambda: fold_copy(1, slab, block).wait_recv())

    right_lanes = lax.broadcasted_iota(jnp.int32, (half, LANE), 1) >= BLOCK

    def local(block, slab, p, part):
        tiles = [gathered(2 * slab + p, 2 * part + 1 + t, block) for t in range(2)]
        side, edge = (1, 0) if part == 0 else (0, 1)
        packed = took[side, slab, block, p]
        turned = pltpu.roll(packed, BLOCK, 1)
        zero = jnp.zeros_like(packed)
        if part == 0:
            pieces = [jnp.where(right_lanes, zero, packed), jnp.where(right_lanes, zero, turned)]
        else:
            pieces = [jnp.where(right_lanes, packed, zero), jnp.where(right_lanes, turned, zero)]
        tiles[edge] = tiles[edge] + jnp.concatenate(pieces, 0)
        return tiles

    sent = []

    def rim_copy(chain, step, slab, source):
        return remote(
            source, rim_slot.at[chain, step, slab],
            rim_send.at[chain, step, slab], rim_recv.at[chain, step, slab], (r, c, around(CHAINS[chain][0])),
        )

    def main_copy(chain, step, slab, source):
        return remote(
            source, slot.at[chain, step, slab],
            main_send.at[chain, step, slab], main_recv.at[chain, step, slab], (r, c, around(CHAINS[chain][0])),
        )

    own = piece_rows(0, z)

    def rim_load(slab):
        for index, block in enumerate((0, blocks - 1)):
            await_fold(slab, block)
            for part in range(2):
                for p in range(2):
                    for t, tile in enumerate(local(block, slab, p, part)):
                        rim[part, slab, index, p, t] = tile

    def rim_round(k, slab):
        for chain, (direction, part, length) in enumerate(CHAINS):
            step = k - (FAR - length)
            if step < 0:
                continue
            piece = piece_rows(0, around(direction * (FAR - k)))
            if step == 0:
                source = rim.at[part, slab, :, :, :, piece, :]
            else:
                source = rim_slot.at[chain, step - 1, slab]
                rim_copy(chain, step - 1, slab, source).wait_recv()
                source[...] += rim[part, slab, :, :, :, piece, :]
            copy = rim_copy(chain, step, slab, source)
            copy.start()
            sent.append(copy)

    def main_round(k, slab):
        for offset in ((4,), (3, -3), (2, -2), (1, -1))[k]:
            await_fold(slab, around(offset) + 1)
        for chain, (direction, part, length) in enumerate(CHAINS):
            step = k - (FAR - length)
            if step < 0:
                continue
            block = around(direction * (FAR - k)) + 1
            if step == 0:
                source = stage.at[chain, slab]
            else:
                source = slot.at[chain, step - 1, slab]
                main_copy(chain, step - 1, slab, source).wait_recv()
            for p in range(2):
                for t, tile in enumerate(local(block, slab, p, part)):
                    if step == 0:
                        source[p, t] = tile
                    else:
                        source[p, t] += tile
            copy = main_copy(chain, step, slab, source)
            copy.start()
            sent.append(copy)

    def ends(part):
        return [(chain, length - 1) for chain, (_, q, length) in enumerate(CHAINS) if q == part]

    def far_copy(side, slab):
        target = (r - 1, c, last) if side == 0 else (r + 1, c, 0)
        return remote(
            rim_sum.at[slab, side], far.at[slab, :, :, own, :], far_send.at[slab, side], far_recv.at[slab, z], target
        )

    def rim_end(slab):
        for part in range(2):
            (a, i), (b, j) = ends(part)
            for chain, step in ((a, i), (b, j)):
                rim_copy(chain, step, slab, rim_slot.at[chain, step, slab]).wait_recv()
            total = rim[part, slab, :, :, :, own, :] + rim_slot[a, i, slab] + rim_slot[b, j, slab]
            rim_sum[slab, :, :, 2 * part : 2 * part + 2] = total
        pl.when(has_up)(lambda: far_copy(0, slab).start())
        pl.when(has_down)(lambda: far_copy(1, slab).start())

    takes = jnp.logical_or(jnp.logical_and(z == last, has_down), jnp.logical_and(z == 0, has_up))

    def finish(slab):
        await_fold(slab, z + 1)
        for part in range(2):
            (a, i), (b, j) = ends(part)
            for chain, step in ((a, i), (b, j)):
                main_copy(chain, step, slab, slot.at[chain, step, slab]).wait_recv()
            for p in range(2):
                tiles = local(z + 1, slab, p, part)
                for t in range(2):
                    out_ref[2 * slab + p, :, (2 * part + t) * LANE : (2 * part + t + 1) * LANE] = (
                        tiles[t] + slot[a, i, slab, p, t] + slot[b, j, slab, p, t]
                    )

        @pl.when(takes)
        def _():
            for other in range(depth):
                remote(
                    rim_sum.at[slab, 0], far.at[slab, :, :, other * PIECE : (other + 1) * PIECE, :],
                    far_send.at[slab, 0], far_recv.at[slab, other], (r, c, around(1)),
                ).wait_recv()
            for p in range(2):
                for t in range(4):
                    out_ref[2 * slab + p, :, t * LANE : (t + 1) * LANE] += far[slab, p, t]

    pl.when(jnp.logical_not(has_right))(lambda: took.__setitem__(0, jnp.zeros_like(took[0])))
    pl.when(jnp.logical_not(has_left))(lambda: took.__setitem__(1, jnp.zeros_like(took[1])))

    lax.fori_loop(0, PMAX, outward, 0)
    fold(1)
    rim_load(1)
    rim_round(0, 1)
    main_round(0, 1)
    lax.fori_loop(0, PMAX, inward, 0)
    fold(0)
    rim_round(1, 1)
    rim_load(0)
    rim_round(0, 0)
    main_round(0, 0)
    rim_round(2, 1)
    main_round(1, 1)
    rim_round(1, 0)
    rim_round(3, 1)
    rim_round(2, 0)
    main_round(1, 0)
    rim_end(1)
    rim_round(3, 0)
    main_round(2, 1)
    rim_end(0)
    main_round(2, 0)
    main_round(3, 1)
    main_round(3, 0)
    finish(1)
    finish(0)

    for copy in sent:
        copy.wait_send()
    for slab in range(2):
        pl.when(has_up)(lambda: far_copy(0, slab).wait_send())
        pl.when(has_down)(lambda: far_copy(1, slab).wait_send())
    for side in range(2):

        @pl.when((has_left, has_right)[side])
        def _():
            for slab in range(2):
                for block in range(blocks):
                    fold_copy(side, slab, block).wait_send()
            side_copy(1 - side).wait_send()

        @pl.when((has_down, has_up)[side])
        def _():
            row_copy(side).wait_send()

        @pl.when(live[side])
        def _():
            for at, part, offset, index in corners:
                if at == side:
                    pl.when(targets[part][0])(lambda: corner_copy(side, part, offset, index).wait_send())
            for chain, (_, _, length) in enumerate(CHAINS):
                for step in range(length):
                    ring_copy(side, chain, step).wait_send()


def fused_call(sizes, count, corners, field, phase, probe, halves, measured):
    planes, core, _ = field.shape
    depth = sizes[2]
    reach = core + 2 * HALO
    blocks = reach // BLOCK
    f32, bf16 = jnp.float32, jnp.bfloat16
    dma = pltpu.SemaphoreType.DMA
    smem = pl.BlockSpec(memory_space=pltpu.SMEM)
    return pl.pallas_call(
        functools.partial(fused_kernel, sizes),
        out_shape=jax.ShapeDtypeStruct((planes, BLOCK, core), f32),
        in_specs=[smem, smem] + [pl.BlockSpec(memory_space=pltpu.HBM)] * 5,
        out_specs=pl.BlockSpec(memory_space=pltpu.VMEM),
        scratch_shapes=[
            pltpu.VMEM((planes, 6, reach, LANE), f32),
            pltpu.VMEM((2, PATCH, PATCH), f32),
            pltpu.VMEM((2, PATCH, PATCH), f32),
            pltpu.VMEM((PMAX, PATCH, PATCH), f32),
            pltpu.VMEM((2 * PATCH, 2 * PATCH), bf16),
            pltpu.VMEM((2 * PATCH, 2 * PATCH), bf16),
            pltpu.VMEM((2, PATCH, PATCH), bf16),
            pltpu.VMEM((PMAX, 2 * PATCH, PATCH), bf16),
            pltpu.VMEM((PMAX, planes, 5, PATCH + 2 * BLOCK, LANE), f32),
            pltpu.VMEM((2, 2, blocks, 2, BLOCK // 2, LANE), f32),
            pltpu.VMEM((2, 2, blocks, 2, BLOCK // 2, LANE), f32),
            pltpu.VMEM((4, 2, 2, 2, BLOCK, LANE), f32),
            pltpu.VMEM((2, 2, 2, 2, 2, BLOCK, LANE), f32),
            pltpu.VMEM((4, FAR, 2, 2, 2, 2, PIECE, LANE), f32),
            pltpu.VMEM((4, FAR, 2, 2, 2, BLOCK, LANE), f32),
            pltpu.VMEM((2, 2, 2, 4, PIECE, LANE), f32),
            pltpu.VMEM((2, 2, 4, BLOCK, LANE), f32),
            dma((4,)), dma((4,)), dma((2,)), dma((2,)), dma((2, 4, FAR)), dma((2, 4, FAR)),
            dma((2,)), dma((2,)), dma((2, 2, depth)), dma((2, 2, depth)),
            dma((2, 2, blocks)), dma((2, 2, blocks)), dma((4, FAR, 2)), dma((4, FAR, 2)),
            dma((4, FAR, 2)), dma((4, FAR, 2)), dma((2, 2)), dma((2, depth)),
        ],
        compiler_params=pltpu.CompilerParams(
            collective_id=0, has_side_effects=True, vmem_limit_bytes=63 << 20
        ),
    )(count, corners, field, phase, probe, halves, measured)


def shards(sizes, object_field, probe_field, prop_phase, measured, positions, counts):
    gradient = fused_call(
        sizes,
        counts.reshape(1),
        positions.reshape(PMAX, 2).T,
        object_field.reshape(4, *object_field.shape[2:]),
        prop_phase,
        probe_field,
        jnp.asarray(dft_halves()),
        measured.reshape(PMAX, PATCH, PATCH),
    )
    return gradient.reshape(2, 2, *gradient.shape[1:])


def solution(mesh):
    placed = (
        P(None, None, "row", "col"),
        P(),
        P(),
        P("row", "col", "scan", None, None, None),
        P("row", "col", "scan", None, None),
        P("row", "col", "scan"),
    )
    sizes = tuple(mesh.shape[name] for name in ("row", "col", "scan"))
    return jax.shard_map(
        functools.partial(shards, sizes),
        mesh=mesh,
        in_specs=placed,
        out_specs=P(None, None, ("row", "scan"), "col"),
        check_vma=False,
    )
```

```python
import functools
import math

import jax
import jax.numpy as jnp
import numpy as np
from jax import lax
from jax.experimental import pallas as pl
from jax.experimental.pallas import tpu as pltpu
from jax.sharding import PartitionSpec as P

PATCH = 256
HALO = 64
PMAX = 3
LANE = 128
BLOCK = 64
PIECE = 8
FAR = 4
CHAINS = ((1, 0, 3), (1, 1, 4), (-1, 0, 4), (-1, 1, 3))
MESH = pl.DeviceIdType.MESH


def dft_halves():
    k = np.arange(PATCH)
    angles = ((k[:, None] * k[None, :]) % PATCH).astype(np.float32) * np.float32(2.0 * math.pi / PATCH)
    scale = np.float32(math.sqrt(PATCH))
    return np.stack([np.cos(angles) / scale, np.sin(angles) / scale]).astype(jnp.bfloat16)


def stacked(real, imag):
    return jnp.concatenate([real.astype(jnp.bfloat16), imag.astype(jnp.bfloat16)], 0)


def transform(batch, left, right):
    middle = jnp.dot(left, jnp.concatenate(batch, 1), preferred_element_type=jnp.float32).astype(jnp.bfloat16)
    spans = [slice(k * PATCH, (k + 1) * PATCH) for k in range(len(batch))]
    wide = jnp.concatenate([jnp.concatenate([middle[:PATCH, at], middle[PATCH:, at]], 1) for at in spans], 0)
    out = jnp.dot(wide, right, preferred_element_type=jnp.float32)
    return [(out[at, :PATCH], out[at, PATCH:]) for at in spans]


def fused_kernel(
    sizes, count_ref, corner_ref, field_ref, phase_ref, probe_hbm, half_ref, measured_hbm, out_ref,
    ext_ref, prop_ref, probe_ref, measured_ref, fwd_ref, inv_ref, halves, through, placed,
    pack, took, stage, rim, rim_slot, slot, rim_sum, far,
    load_sem, core_sem, row_send, row_recv, ring_send, ring_recv, side_send, side_recv, corner_send, corner_recv,
    fold_send, fold_recv, rim_send, rim_recv, main_send, main_recv, far_send, far_recv,
):
    rows, cols, depth = sizes
    r, c, z = (lax.axis_index(name) for name in ("row", "col", "scan"))
    last = depth - 1
    has_left, has_right = c > 0, c < cols - 1
    has_up, has_down = r > 0, r < rows - 1
    core = field_ref.shape[1]
    blocks = ext_ref.shape[2] // BLOCK
    half = BLOCK // 2

    def around(step):
        return lax.rem(z + (step + depth), depth)

    def remote(source, target, send, recv, device):
        return pltpu.make_async_remote_copy(
            src_ref=source, dst_ref=target, send_sem=send, recv_sem=recv, device_id=device, device_id_type=MESH
        )

    barrier = pltpu.get_barrier_semaphore()

    def greet(device):
        pl.semaphore_signal(barrier, inc=1, device_id=device, device_id_type=MESH)

    pl.when(has_up)(lambda: greet((r - 1, c, z)))
    pl.when(has_down)(lambda: greet((r + 1, c, z)))
    pl.when(has_left)(lambda: greet((r, c - 1, z)))
    pl.when(has_right)(lambda: greet((r, c + 1, z)))
    for step in (1, -1):
        greet((r, c, around(step)))

    fills = [
        pltpu.make_async_copy(
            field_ref.at[:, :, t * LANE : (t + 1) * LANE], ext_ref.at[:, t + 1, HALO : HALO + core, :], core_sem.at[t]
        )
        for t in range(4)
    ]
    for fill in fills:
        fill.start()
    pairs = ((phase_ref, prop_ref.at[0]), (half_ref, halves), (probe_hbm, probe_ref), (measured_hbm, measured_ref))
    loads = [pltpu.make_async_copy(source, target, load_sem.at[i]) for i, (source, target) in enumerate(pairs)]
    for load in loads:
        load.start()
    for fill in fills:
        fill.wait()
    count = jnp.int32(2)
    for flag in (has_left, has_right, has_up, has_down):
        count = count + flag.astype(jnp.int32)
    pl.semaphore_wait(barrier, count)

    def piece_rows(first, piece):
        return pl.ds(pl.multiple_of(first + piece * PIECE, PIECE), PIECE)

    starts = (0, HALO + core)

    def row_copy(side):
        source = piece_rows(core if side == 0 else HALO, z)
        return remote(
            ext_ref.at[:, 1:5, source, :], ext_ref.at[:, 1:5, piece_rows(starts[side], z), :],
            row_send.at[side], row_recv.at[side], (r + 1 - 2 * side, c, z),
        )

    def side_copy(side):
        tile, target = ((4, 0), (1, 5))[side]
        return remote(
            ext_ref.at[:, tile, HALO : HALO + core, :], ext_ref.at[:, target, HALO : HALO + core, :],
            side_send.at[side], side_recv.at[side], (r, c + 1 - 2 * side, z),
        )

    def ring_copy(side, chain, step):
        direction, part, _ = CHAINS[chain]
        place = ext_ref.at[:, 2 * part + 1 : 2 * part + 3, piece_rows(starts[side], around(-direction * step)), :]
        return remote(
            place, place, ring_send.at[side, chain, step], ring_recv.at[side, chain, step], (r, c, around(direction))
        )

    def corner_copy(side, part, offset, index):
        tile, target = ((1, 5), (4, 0))[part]
        place = piece_rows(starts[side], around(offset))
        return remote(
            ext_ref.at[:, tile, place, :], ext_ref.at[:, target, place, :],
            corner_send.at[side, part, index], corner_recv.at[side, part, index], (r, c + 2 * part - 1, z),
        )

    pl.when(has_down)(lambda: row_copy(0).start())
    pl.when(has_up)(lambda: row_copy(1).start())

    loads[0].wait()
    phase = prop_ref[0]
    prop_ref[0] = jnp.cos(phase)
    prop_ref[1] = jnp.sin(phase)
    loads[1].wait()
    cosines, sines = halves[0], halves[1]
    for ref, above, below in ((fwd_ref, sines, -sines), (inv_ref, -sines, sines)):
        ref[:PATCH, :PATCH] = cosines
        ref[PATCH:, PATCH:] = cosines
        ref[:PATCH, PATCH:] = above
        ref[PATCH:, :PATCH] = below

    targets = ((has_left, has_right), (has_right, has_left))
    live = (has_up, has_down)
    corners = []

    def send_corner(side, part, offset):
        index = len([1 for entry in corners if entry[:2] == (side, part)])
        corners.append((side, part, offset, index))
        pl.when(targets[part][0])(lambda: corner_copy(side, part, offset, index).start())

    for step in range(FAR + 1):
        for side in range(2):

            @pl.when(live[side])
            def _():
                if step == 0:
                    row_copy(side).wait_recv()
                for chain, (direction, part, length) in enumerate(CHAINS):
                    if 0 < step <= length:
                        ring_copy(side, chain, step - 1).wait_recv()
                    if step < length:
                        ring_copy(side, chain, step).start()
                for chain, (direction, part, length) in enumerate(CHAINS):
                    if step == 0 and chain < 2:
                        send_corner(side, chain, 0)
                    if 0 < step <= length:
                        send_corner(side, part, -direction * step)

        if step == 0:
            pl.when(has_right)(lambda: side_copy(0).start())
            pl.when(has_left)(lambda: side_copy(1).start())
            placed[...] = jnp.zeros_like(placed)

    for side in range(2):
        pl.when((has_left, has_right)[side])(lambda: side_copy(side).wait_recv())

        @pl.when(live[side])
        def _():
            for at, part, offset, index in corners:
                if at == side:
                    pl.when(targets[part][1])(lambda: corner_copy(side, part, offset, index).wait_recv())

    for load in loads[2:]:
        load.wait()

    def position(k):
        row = jnp.clip(corner_ref[0, k], -HALO, core + HALO - PATCH) + HALO
        col = jnp.clip(corner_ref[1, k], -HALO, core + HALO - PATCH) + LANE
        tile = lax.shift_right_logical(col, 7)
        return row, tile, col - tile * LANE

    patches = count_ref[0]
    lanes = lax.broadcasted_iota(jnp.int32, (PATCH, LANE), 1)

    def place(k, plane, value, shift):
        late = lanes < shift
        first, second = (pltpu.roll(value[:, t * LANE : (t + 1) * LANE], shift, 1) for t in range(2))
        zero = jnp.zeros_like(first)
        parts = (jnp.where(late, zero, first), jnp.where(late, first, second), jnp.where(late, second, zero))
        for t, tile in enumerate(parts):
            placed[k, plane, t + 1, BLOCK : BLOCK + PATCH, :] = jnp.where(k < patches, tile, 0.0)

    def window(k, plane):
        row, tile, shift = position(k)
        back = lax.rem(LANE - shift, LANE)
        early = lanes < LANE - shift
        turned = [pltpu.roll(ext_ref[plane, tile + t, pl.ds(row, PATCH), :], back, 1) for t in range(3)]
        return jnp.concatenate([jnp.where(early, turned[0], turned[1]), jnp.where(early, turned[1], turned[2])], 1)

    def forward(batch):
        return transform(batch, fwd_ref[...], inv_ref[...])

    def inverse(batch):
        return transform(batch, inv_ref[...], fwd_ref[...])

    def outward():
        pr, pi = probe_ref[0], probe_ref[1]
        hr, hi = prop_ref[0], prop_ref[1]
        batch = []
        for k in range(PMAX):
            ar, ai = window(k, 0), window(k, 1)
            batch.append(stacked(pr * ar - pi * ai, pr * ai + pi * ar))
        arrived = inverse([stacked(hr * sr - hi * si, hr * si + hi * sr) for sr, si in forward(batch)])
        batch = []
        for k, (wr, wi) in enumerate(arrived):
            br, bi = window(k, 2), window(k, 3)
            batch.append(stacked(br * wr - bi * wi, br * wi + bi * wr))
        batch, distant = [], forward(batch)
        for k, (fr, fi) in enumerate(distant):
            level = fr * fr + fi * fi - measured_ref[k]
            batch.append(stacked(level * fr, level * fi))
        for k, ((wr, wi), (gr, gi)) in enumerate(zip(arrived, inverse(batch), strict=True)):
            shift = position(k)[2]
            br, bi = window(k, 2), window(k, 3)
            place(k, 2, wr * gr + wi * gi, shift)
            place(k, 3, wr * gi - wi * gr, shift)
            through[k] = stacked(br * gr + bi * gi, br * gi - bi * gr)

    def inward():
        pr, pi = probe_ref[0], probe_ref[1]
        hr, hi = prop_ref[0], prop_ref[1]
        spectra = forward([through[k] for k in range(PMAX)])
        for k, (qr, qi) in enumerate(inverse([stacked(hr * tr + hi * ti, hr * ti - hi * tr) for tr, ti in spectra])):
            shift = position(k)[2]
            place(k, 0, pr * qr + pi * qi, shift)
            place(k, 1, pr * qi - pi * qr, shift)

    spots = [position(k)[:2] for k in range(PMAX)]

    def gathered(plane, tile, block):
        total = None
        for k, (row, first) in enumerate(spots):
            at = jnp.clip(block * BLOCK - row, -BLOCK, PATCH) + BLOCK
            value = placed[k, plane, jnp.clip(tile - first, -1, 3) + 1, pl.ds(at, BLOCK), :]
            total = value if total is None else total + value
        return total

    def fold_copy(side, slab, block):
        return remote(
            pack.at[side, slab, block], took.at[side, slab, block],
            fold_send.at[side, slab, block], fold_recv.at[side, slab, block], (r, c + (2 * side - 1), z),
        )

    def fold(slab):
        steps = (4, 3, -3, 2, -2, 1, -1, 0)
        for block in [0, blocks - 1] + [around(step) + 1 for step in steps]:
            for side, tile in ((0, 0), (1, 5)):
                for p in range(2):
                    whole = gathered(2 * slab + p, tile, block)
                    pack[side, slab, block, p] = whole[:half] + pltpu.roll(whole[half:], BLOCK, 1)
            pl.when(has_left)(lambda: fold_copy(0, slab, block).start())
            pl.when(has_right)(lambda: fold_copy(1, slab, block).start())

    def await_fold(slab, block):
        pl.when(has_right)(lambda: fold_copy(0, slab, block).wait_recv())
        pl.when(has_left)(lambda: fold_copy(1, slab, block).wait_recv())

    right_lanes = lax.broadcasted_iota(jnp.int32, (half, LANE), 1) >= BLOCK

    def local(block, slab, p, part):
        tiles = [gathered(2 * slab + p, 2 * part + 1 + t, block) for t in range(2)]
        side, edge = (1, 0) if part == 0 else (0, 1)
        packed = took[side, slab, block, p]
        turned = pltpu.roll(packed, BLOCK, 1)
        zero = jnp.zeros_like(packed)
        if part == 0:
            pieces = [jnp.where(right_lanes, zero, packed), jnp.where(right_lanes, zero, turned)]
        else:
            pieces = [jnp.where(right_lanes, packed, zero), jnp.where(right_lanes, turned, zero)]
        tiles[edge] = tiles[edge] + jnp.concatenate(pieces, 0)
        return tiles

    sent = []

    def rim_copy(chain, step, slab, source):
        return remote(
            source, rim_slot.at[chain, step, slab],
            rim_send.at[chain, step, slab], rim_recv.at[chain, step, slab], (r, c, around(CHAINS[chain][0])),
        )

    def main_copy(chain, step, slab, source):
        return remote(
            source, slot.at[chain, step, slab],
            main_send.at[chain, step, slab], main_recv.at[chain, step, slab], (r, c, around(CHAINS[chain][0])),
        )

    own = piece_rows(0, z)

    def rim_load(slab):
        for index, block in enumerate((0, blocks - 1)):
            await_fold(slab, block)
            for part in range(2):
                for p in range(2):
                    for t, tile in enumerate(local(block, slab, p, part)):
                        rim[part, slab, index, p, t] = tile

    def rim_round(k, slab):
        for chain, (direction, part, length) in enumerate(CHAINS):
            step = k - (FAR - length)
            if step < 0:
                continue
            piece = piece_rows(0, around(direction * (FAR - k)))
            if step == 0:
                source = rim.at[part, slab, :, :, :, piece, :]
            else:
                source = rim_slot.at[chain, step - 1, slab]
                rim_copy(chain, step - 1, slab, source).wait_recv()
                source[...] += rim[part, slab, :, :, :, piece, :]
            copy = rim_copy(chain, step, slab, source)
            copy.start()
            sent.append(copy)

    def main_round(k, slab):
        for offset in ((4,), (3, -3), (2, -2), (1, -1))[k]:
            await_fold(slab, around(offset) + 1)
        for chain, (direction, part, length) in enumerate(CHAINS):
            step = k - (FAR - length)
            if step < 0:
                continue
            block = around(direction * (FAR - k)) + 1
            if step == 0:
                source = stage.at[chain, slab]
            else:
                source = slot.at[chain, step - 1, slab]
                main_copy(chain, step - 1, slab, source).wait_recv()
            for p in range(2):
                for t, tile in enumerate(local(block, slab, p, part)):
                    if step == 0:
                        source[p, t] = tile
                    else:
                        source[p, t] += tile
            copy = main_copy(chain, step, slab, source)
            copy.start()
            sent.append(copy)

    def ends(part):
        return [(chain, length - 1) for chain, (_, q, length) in enumerate(CHAINS) if q == part]

    def far_copy(side, slab):
        target = (r - 1, c, last) if side == 0 else (r + 1, c, 0)
        return remote(
            rim_sum.at[slab, side], far.at[slab, :, :, own, :], far_send.at[slab, side], far_recv.at[slab, z], target
        )

    def rim_end(slab):
        for part in range(2):
            (a, i), (b, j) = ends(part)
            for chain, step in ((a, i), (b, j)):
                rim_copy(chain, step, slab, rim_slot.at[chain, step, slab]).wait_recv()
            total = rim[part, slab, :, :, :, own, :] + rim_slot[a, i, slab] + rim_slot[b, j, slab]
            rim_sum[slab, :, :, 2 * part : 2 * part + 2] = total
        pl.when(has_up)(lambda: far_copy(0, slab).start())
        pl.when(has_down)(lambda: far_copy(1, slab).start())

    takes = jnp.logical_or(jnp.logical_and(z == last, has_down), jnp.logical_and(z == 0, has_up))

    def finish(slab):
        await_fold(slab, z + 1)
        for part in range(2):
            (a, i), (b, j) = ends(part)
            for chain, step in ((a, i), (b, j)):
                main_copy(chain, step, slab, slot.at[chain, step, slab]).wait_recv()
            for p in range(2):
                tiles = local(z + 1, slab, p, part)
                for t in range(2):
                    out_ref[2 * slab + p, :, (2 * part + t) * LANE : (2 * part + t + 1) * LANE] = (
                        tiles[t] + slot[a, i, slab, p, t] + slot[b, j, slab, p, t]
                    )

        @pl.when(takes)
        def _():
            for other in range(depth):
                remote(
                    rim_sum.at[slab, 0], far.at[slab, :, :, other * PIECE : (other + 1) * PIECE, :],
                    far_send.at[slab, 0], far_recv.at[slab, other], (r, c, around(1)),
                ).wait_recv()
            for p in range(2):
                for t in range(4):
                    out_ref[2 * slab + p, :, t * LANE : (t + 1) * LANE] += far[slab, p, t]

    pl.when(jnp.logical_not(has_right))(lambda: took.__setitem__(0, jnp.zeros_like(took[0])))
    pl.when(jnp.logical_not(has_left))(lambda: took.__setitem__(1, jnp.zeros_like(took[1])))

    outward()
    fold(1)
    inward()
    fold(0)
    rim_load(1)
    rim_round(0, 1)
    main_round(0, 1)
    rim_load(0)
    rim_round(0, 0)
    main_round(0, 0)
    rim_round(1, 1)
    rim_round(1, 0)
    main_round(1, 1)
    rim_round(2, 1)
    rim_round(2, 0)
    main_round(1, 0)
    rim_round(3, 1)
    rim_round(3, 0)
    main_round(2, 1)
    rim_end(1)
    rim_end(0)
    main_round(2, 0)
    main_round(3, 1)
    main_round(3, 0)
    finish(1)
    finish(0)

    for copy in sent:
        copy.wait_send()
    for slab in range(2):
        pl.when(has_up)(lambda: far_copy(0, slab).wait_send())
        pl.when(has_down)(lambda: far_copy(1, slab).wait_send())
    for side in range(2):

        @pl.when((has_left, has_right)[side])
        def _():
            for slab in range(2):
                for block in range(blocks):
                    fold_copy(side, slab, block).wait_send()
            side_copy(1 - side).wait_send()

        @pl.when((has_down, has_up)[side])
        def _():
            row_copy(side).wait_send()

        @pl.when(live[side])
        def _():
            for at, part, offset, index in corners:
                if at == side:
                    pl.when(targets[part][0])(lambda: corner_copy(side, part, offset, index).wait_send())
            for chain, (_, _, length) in enumerate(CHAINS):
                for step in range(length):
                    ring_copy(side, chain, step).wait_send()


def fused_call(sizes, count, corners, field, phase, probe, halves, measured):
    planes, core, _ = field.shape
    depth = sizes[2]
    reach = core + 2 * HALO
    blocks = reach // BLOCK
    f32, bf16 = jnp.float32, jnp.bfloat16
    dma = pltpu.SemaphoreType.DMA
    smem = pl.BlockSpec(memory_space=pltpu.SMEM)
    return pl.pallas_call(
        functools.partial(fused_kernel, sizes),
        out_shape=jax.ShapeDtypeStruct((planes, BLOCK, core), f32),
        in_specs=[smem, smem] + [pl.BlockSpec(memory_space=pltpu.HBM)] * 5,
        out_specs=pl.BlockSpec(memory_space=pltpu.VMEM),
        scratch_shapes=[
            pltpu.VMEM((planes, 6, reach, LANE), f32),
            pltpu.VMEM((2, PATCH, PATCH), f32),
            pltpu.VMEM((2, PATCH, PATCH), f32),
            pltpu.VMEM((PMAX, PATCH, PATCH), f32),
            pltpu.VMEM((2 * PATCH, 2 * PATCH), bf16),
            pltpu.VMEM((2 * PATCH, 2 * PATCH), bf16),
            pltpu.VMEM((2, PATCH, PATCH), bf16),
            pltpu.VMEM((PMAX, 2 * PATCH, PATCH), bf16),
            pltpu.VMEM((PMAX, planes, 5, PATCH + 2 * BLOCK, LANE), f32),
            pltpu.VMEM((2, 2, blocks, 2, BLOCK // 2, LANE), f32),
            pltpu.VMEM((2, 2, blocks, 2, BLOCK // 2, LANE), f32),
            pltpu.VMEM((4, 2, 2, 2, BLOCK, LANE), f32),
            pltpu.VMEM((2, 2, 2, 2, 2, BLOCK, LANE), f32),
            pltpu.VMEM((4, FAR, 2, 2, 2, 2, PIECE, LANE), f32),
            pltpu.VMEM((4, FAR, 2, 2, 2, BLOCK, LANE), f32),
            pltpu.VMEM((2, 2, 2, 4, PIECE, LANE), f32),
            pltpu.VMEM((2, 2, 4, BLOCK, LANE), f32),
            dma((4,)), dma((4,)), dma((2,)), dma((2,)), dma((2, 4, FAR)), dma((2, 4, FAR)),
            dma((2,)), dma((2,)), dma((2, 2, depth)), dma((2, 2, depth)),
            dma((2, 2, blocks)), dma((2, 2, blocks)), dma((4, FAR, 2)), dma((4, FAR, 2)),
            dma((4, FAR, 2)), dma((4, FAR, 2)), dma((2, 2)), dma((2, depth)),
        ],
        compiler_params=pltpu.CompilerParams(
            collective_id=0, has_side_effects=True, vmem_limit_bytes=63 << 20
        ),
    )(count, corners, field, phase, probe, halves, measured)


def shards(sizes, object_field, probe_field, prop_phase, measured, positions, counts):
    gradient = fused_call(
        sizes,
        counts.reshape(1),
        positions.reshape(PMAX, 2).T,
        object_field.reshape(4, *object_field.shape[2:]),
        prop_phase,
        probe_field,
        jnp.asarray(dft_halves()),
        measured.reshape(PMAX, PATCH, PATCH),
    )
    return gradient.reshape(2, 2, *gradient.shape[1:])


def solution(mesh):
    placed = (
        P(None, None, "row", "col"),
        P(),
        P(),
        P("row", "col", "scan", None, None, None),
        P("row", "col", "scan", None, None),
        P("row", "col", "scan"),
    )
    sizes = tuple(mesh.shape[name] for name in ("row", "col", "scan"))
    return jax.shard_map(
        functools.partial(shards, sizes),
        mesh=mesh,
        in_specs=placed,
        out_specs=P(None, None, ("row", "scan"), "col"),
        check_vma=False,
    )
```

```python
import functools
import math

import jax
import jax.numpy as jnp
import numpy as np
from jax import lax
from jax.experimental import pallas as pl
from jax.experimental.pallas import tpu as pltpu
from jax.sharding import PartitionSpec as P

PATCH = 256
HALO = 64
PMAX = 3
LANE = 128
BLOCK = 64
PIECE = 8
FAR = 4
CHAINS = ((1, 0, 3), (1, 1, 4), (-1, 0, 4), (-1, 1, 3))
WAYS = (1, -1)
MESH = pl.DeviceIdType.MESH


def dft_halves():
    k = np.arange(PATCH)
    angles = ((k[:, None] * k[None, :]) % PATCH).astype(np.float32) * np.float32(2.0 * math.pi / PATCH)
    scale = np.float32(math.sqrt(PATCH))
    return np.stack([np.cos(angles) / scale, np.sin(angles) / scale]).astype(jnp.bfloat16)


def stacked(real, imag):
    return jnp.concatenate([real.astype(jnp.bfloat16), imag.astype(jnp.bfloat16)], 0)


def transform(batch, left, right):
    middle = jnp.dot(left, jnp.concatenate(batch, 1), preferred_element_type=jnp.float32).astype(jnp.bfloat16)
    spans = [slice(k * PATCH, (k + 1) * PATCH) for k in range(len(batch))]
    wide = jnp.concatenate([jnp.concatenate([middle[:PATCH, at], middle[PATCH:, at]], 1) for at in spans], 0)
    out = jnp.dot(wide, right, preferred_element_type=jnp.float32)
    return [(out[at, :PATCH], out[at, PATCH:]) for at in spans]


def fused_kernel(
    sizes, count_ref, corner_ref, field_ref, phase_ref, probe_hbm, half_ref, measured_hbm, out_ref,
    ext_first, ext_second, prop_ref, probe_ref, measured_ref, fwd_ref, inv_ref, halves, through, placed,
    pack, took, stage, rim, rim_slot, slot, rim_sum, far,
    load_sem, core_sem, row_send, row_recv, ring_send, ring_recv, side_send, side_recv, corner_send, corner_recv,
    fold_send, fold_recv, rim_send, rim_recv, main_send, main_recv, far_send, far_recv,
):
    rows, cols, depth = sizes
    r, c, z = (lax.axis_index(name) for name in ("row", "col", "scan"))
    last = depth - 1
    has_left, has_right = c > 0, c < cols - 1
    has_up, has_down = r > 0, r < rows - 1
    core = field_ref.shape[1]
    exts = (ext_first, ext_second)
    blocks = ext_first.shape[2] // BLOCK
    half = BLOCK // 2

    def around(step):
        return lax.rem(z + (step + depth), depth)

    def remote(source, target, send, recv, device):
        return pltpu.make_async_remote_copy(
            src_ref=source, dst_ref=target, send_sem=send, recv_sem=recv, device_id=device, device_id_type=MESH
        )

    barrier = pltpu.get_barrier_semaphore()

    def greet(device):
        pl.semaphore_signal(barrier, inc=1, device_id=device, device_id_type=MESH)

    pl.when(has_up)(lambda: greet((r - 1, c, z)))
    pl.when(has_down)(lambda: greet((r + 1, c, z)))
    pl.when(has_left)(lambda: greet((r, c - 1, z)))
    pl.when(has_right)(lambda: greet((r, c + 1, z)))
    for step in (1, -1):
        greet((r, c, around(step)))

    fills = [
        pltpu.make_async_copy(
            field_ref.at[2 * slab : 2 * slab + 2, :, t * LANE : (t + 1) * LANE],
            exts[slab].at[:, t + 1, HALO : HALO + core, :],
            core_sem.at[slab, t],
        )
        for slab in range(2)
        for t in range(4)
    ]
    for fill in fills:
        fill.start()
    pairs = ((phase_ref, prop_ref.at[0]), (half_ref, halves), (probe_hbm, probe_ref), (measured_hbm, measured_ref))
    loads = [pltpu.make_async_copy(source, target, load_sem.at[i]) for i, (source, target) in enumerate(pairs)]
    for load in loads:
        load.start()
    for fill in fills:
        fill.wait()
    count = jnp.int32(2)
    for flag in (has_left, has_right, has_up, has_down):
        count = count + flag.astype(jnp.int32)
    pl.semaphore_wait(barrier, count)

    def piece_rows(first, piece):
        return pl.ds(pl.multiple_of(first + piece * PIECE, PIECE), PIECE)

    starts = (0, HALO + core)

    def row_copy(side, slab):
        source = piece_rows(core if side == 0 else HALO, z)
        return remote(
            exts[slab].at[:, 1:5, source, :],
            exts[slab].at[:, 1:5, piece_rows(starts[side], z), :],
            row_send.at[side, slab], row_recv.at[side, slab], (r + 1 - 2 * side, c, z),
        )

    def side_copy(side, slab):
        tile, target = ((4, 0), (1, 5))[side]
        return remote(
            exts[slab].at[:, tile, HALO : HALO + core, :],
            exts[slab].at[:, target, HALO : HALO + core, :],
            side_send.at[side, slab], side_recv.at[side, slab], (r, c + 1 - 2 * side, z),
        )

    def ring_copy(side, chain, step, slab):
        direction, part, _ = CHAINS[chain]
        rows_at = piece_rows(starts[side], around(-direction * step))
        place = exts[slab].at[:, 2 * part + 1 : 2 * part + 3, rows_at, :]
        return remote(
            place, place,
            ring_send.at[side, chain, step, slab], ring_recv.at[side, chain, step, slab], (r, c, around(direction)),
        )

    def corner_copy(side, part, offset, index, slab):
        tile, target = ((1, 5), (4, 0))[part]
        rows_at = piece_rows(starts[side], around(offset))
        return remote(
            exts[slab].at[:, tile, rows_at, :], exts[slab].at[:, target, rows_at, :],
            corner_send.at[side, part, index, slab], corner_recv.at[side, part, index, slab], (r, c + 2 * part - 1, z),
        )

    for slab in range(2):
        pl.when(has_down)(lambda: row_copy(0, slab).start())
        pl.when(has_up)(lambda: row_copy(1, slab).start())

    loads[0].wait()
    phase = prop_ref[0]
    prop_ref[0] = jnp.cos(phase)
    prop_ref[1] = jnp.sin(phase)
    loads[1].wait()
    cosines, sines = halves[0], halves[1]
    for ref, above, below in ((fwd_ref, sines, -sines), (inv_ref, -sines, sines)):
        ref[:PATCH, :PATCH] = cosines
        ref[PATCH:, PATCH:] = cosines
        ref[:PATCH, PATCH:] = above
        ref[PATCH:, :PATCH] = below

    targets = ((has_left, has_right), (has_right, has_left))
    live = (has_up, has_down)
    corners = []

    def send_corner(side, part, offset, slab):
        index = len([1 for entry in corners if entry[:2] == (side, part) and entry[4] == slab])
        corners.append((side, part, offset, index, slab))
        pl.when(targets[part][0])(lambda: corner_copy(side, part, offset, index, slab).start())

    def ring_step(step, slab):
        for side in range(2):

            @pl.when(live[side])
            def _():
                if step == 0:
                    row_copy(side, slab).wait_recv()
                for chain, (direction, part, length) in enumerate(CHAINS):
                    if 0 < step <= length:
                        ring_copy(side, chain, step - 1, slab).wait_recv()
                    if step < length:
                        ring_copy(side, chain, step, slab).start()
                for chain, (direction, part, length) in enumerate(CHAINS):
                    if step == 0 and chain < 2:
                        send_corner(side, chain, 0, slab)
                    if 0 < step <= length:
                        send_corner(side, part, -direction * step, slab)

        if step == 0:
            pl.when(has_right)(lambda: side_copy(0, slab).start())
            pl.when(has_left)(lambda: side_copy(1, slab).start())

    def await_halo(slab):
        for side in range(2):
            pl.when((has_left, has_right)[side])(lambda: side_copy(side, slab).wait_recv())

            @pl.when(live[side])
            def _():
                for at, part, offset, index, which in corners:
                    if at == side and which == slab:
                        pl.when(targets[part][1])(lambda: corner_copy(side, part, offset, index, slab).wait_recv())

    ring_step(0, 0)
    placed[...] = jnp.zeros_like(placed)
    ring_step(0, 1)
    ring_step(1, 0)
    ring_step(2, 0)
    ring_step(1, 1)
    ring_step(3, 0)
    ring_step(2, 1)
    ring_step(4, 0)
    ring_step(3, 1)
    for load in loads[2:]:
        load.wait()
    await_halo(0)

    def position(k):
        row = jnp.clip(corner_ref[0, k], -HALO, core + HALO - PATCH) + HALO
        col = jnp.clip(corner_ref[1, k], -HALO, core + HALO - PATCH) + LANE
        tile = lax.shift_right_logical(col, 7)
        return row, tile, col - tile * LANE

    patches = count_ref[0]
    lanes = lax.broadcasted_iota(jnp.int32, (PATCH, LANE), 1)

    def place(k, plane, value, shift):
        late = lanes < shift
        first, second = (pltpu.roll(value[:, t * LANE : (t + 1) * LANE], shift, 1) for t in range(2))
        zero = jnp.zeros_like(first)
        parts = (jnp.where(late, zero, first), jnp.where(late, first, second), jnp.where(late, second, zero))
        for t, tile in enumerate(parts):
            placed[k, plane, t + 1, BLOCK : BLOCK + PATCH, :] = jnp.where(k < patches, tile, 0.0)

    def window(k, plane):
        row, tile, shift = position(k)
        back = lax.rem(LANE - shift, LANE)
        early = lanes < LANE - shift
        turned = [pltpu.roll(exts[plane // 2][plane % 2, tile + t, pl.ds(row, PATCH), :], back, 1) for t in range(3)]
        return jnp.concatenate([jnp.where(early, turned[0], turned[1]), jnp.where(early, turned[1], turned[2])], 1)

    def forward(batch):
        return transform(batch, fwd_ref[...], inv_ref[...])

    def inverse(batch):
        return transform(batch, inv_ref[...], fwd_ref[...])

    def outward():
        pr, pi = probe_ref[0], probe_ref[1]
        hr, hi = prop_ref[0], prop_ref[1]
        batch = []
        for k in range(PMAX):
            ar, ai = window(k, 0), window(k, 1)
            batch.append(stacked(pr * ar - pi * ai, pr * ai + pi * ar))
        spectra = forward(batch)
        ring_step(4, 1)
        arrived = inverse([stacked(hr * sr - hi * si, hr * si + hi * sr) for sr, si in spectra])
        await_halo(1)
        batch = []
        for k, (wr, wi) in enumerate(arrived):
            br, bi = window(k, 2), window(k, 3)
            batch.append(stacked(br * wr - bi * wi, br * wi + bi * wr))
        batch, distant = [], forward(batch)
        for k, (fr, fi) in enumerate(distant):
            level = fr * fr + fi * fi - measured_ref[k]
            batch.append(stacked(level * fr, level * fi))
        for k, ((wr, wi), (gr, gi)) in enumerate(zip(arrived, inverse(batch), strict=True)):
            shift = position(k)[2]
            br, bi = window(k, 2), window(k, 3)
            place(k, 2, wr * gr + wi * gi, shift)
            place(k, 3, wr * gi - wi * gr, shift)
            through[k] = stacked(br * gr + bi * gi, br * gi - bi * gr)

    def inward():
        pr, pi = probe_ref[0], probe_ref[1]
        hr, hi = prop_ref[0], prop_ref[1]
        spectra = forward([through[k] for k in range(PMAX)])
        for k, (qr, qi) in enumerate(inverse([stacked(hr * tr + hi * ti, hr * ti - hi * tr) for tr, ti in spectra])):
            shift = position(k)[2]
            place(k, 0, pr * qr + pi * qi, shift)
            place(k, 1, pr * qi - pi * qr, shift)

    spots = [position(k)[:2] for k in range(PMAX)]

    def gathered(plane, tile, block):
        total = None
        for k, (row, first) in enumerate(spots):
            at = jnp.clip(block * BLOCK - row, -BLOCK, PATCH) + BLOCK
            value = placed[k, plane, jnp.clip(tile - first, -1, 3) + 1, pl.ds(at, BLOCK), :]
            total = value if total is None else total + value
        return total

    def fold_copy(side, slab, block):
        return remote(
            pack.at[side, slab, block], took.at[side, slab, block],
            fold_send.at[side, slab, block], fold_recv.at[side, slab, block], (r, c + (2 * side - 1), z),
        )

    def fold(slab):
        steps = (4, 3, -3, 2, -2, 1, -1, 0)
        for block in [0, blocks - 1] + [around(step) + 1 for step in steps]:
            for side, tile in ((0, 0), (1, 5)):
                for p in range(2):
                    whole = gathered(2 * slab + p, tile, block)
                    pack[side, slab, block, p] = whole[:half] + pltpu.roll(whole[half:], BLOCK, 1)
            pl.when(has_left)(lambda: fold_copy(0, slab, block).start())
            pl.when(has_right)(lambda: fold_copy(1, slab, block).start())

    def await_fold(slab, block):
        pl.when(has_right)(lambda: fold_copy(0, slab, block).wait_recv())
        pl.when(has_left)(lambda: fold_copy(1, slab, block).wait_recv())

    right_lanes = lax.broadcasted_iota(jnp.int32, (half, LANE), 1) >= BLOCK

    def local(block, slab, p, part):
        tiles = [gathered(2 * slab + p, 2 * part + 1 + t, block) for t in range(2)]
        side, edge = (1, 0) if part == 0 else (0, 1)
        packed = took[side, slab, block, p]
        turned = pltpu.roll(packed, BLOCK, 1)
        zero = jnp.zeros_like(packed)
        if part == 0:
            pieces = [jnp.where(right_lanes, zero, packed), jnp.where(right_lanes, zero, turned)]
        else:
            pieces = [jnp.where(right_lanes, packed, zero), jnp.where(right_lanes, turned, zero)]
        tiles[edge] = tiles[edge] + jnp.concatenate(pieces, 0)
        return tiles

    sent = []

    def rim_copy(chain, step, slab, source):
        return remote(
            source, rim_slot.at[chain, step, slab],
            rim_send.at[chain, step, slab], rim_recv.at[chain, step, slab], (r, c, around(CHAINS[chain][0])),
        )

    def main_copy(chain, step, slab, source):
        return remote(
            source, slot.at[chain, step, slab],
            main_send.at[chain, step, slab], main_recv.at[chain, step, slab], (r, c, around(CHAINS[chain][0])),
        )

    own = piece_rows(0, z)

    def rim_load(slab):
        for index, block in enumerate((0, blocks - 1)):
            await_fold(slab, block)
            for part in range(2):
                for p in range(2):
                    for t, tile in enumerate(local(block, slab, p, part)):
                        rim[part, slab, index, p, t] = tile

    def rim_round(k, slab):
        for chain, (direction, part, length) in enumerate(CHAINS):
            step = k - (FAR - length)
            if step < 0:
                continue
            piece = piece_rows(0, around(direction * (FAR - k)))
            if step == 0:
                source = rim.at[part, slab, :, :, :, piece, :]
            else:
                source = rim_slot.at[chain, step - 1, slab]
                rim_copy(chain, step - 1, slab, source).wait_recv()
                source[...] += rim[part, slab, :, :, :, piece, :]
            copy = rim_copy(chain, step, slab, source)
            copy.start()
            sent.append(copy)

    def main_round(k, slab):
        for offset in ((4,), (3, -3), (2, -2), (1, -1))[k]:
            await_fold(slab, around(offset) + 1)
        for chain, (direction, part, length) in enumerate(CHAINS):
            step = k - (FAR - length)
            if step < 0:
                continue
            block = around(direction * (FAR - k)) + 1
            if step == 0:
                source = stage.at[chain, slab]
            else:
                source = slot.at[chain, step - 1, slab]
                main_copy(chain, step - 1, slab, source).wait_recv()
            for p in range(2):
                for t, tile in enumerate(local(block, slab, p, part)):
                    if step == 0:
                        source[p, t] = tile
                    else:
                        source[p, t] += tile
            copy = main_copy(chain, step, slab, source)
            copy.start()
            sent.append(copy)

    def ends(part):
        return [(chain, length - 1) for chain, (_, q, length) in enumerate(CHAINS) if q == part]

    def far_copy(side, slab):
        target = (r - 1, c, last) if side == 0 else (r + 1, c, 0)
        return remote(
            rim_sum.at[slab, side], far.at[slab, :, :, own, :], far_send.at[slab, side], far_recv.at[slab, z], target
        )

    def rim_end(slab):
        for part in range(2):
            (a, i), (b, j) = ends(part)
            for chain, step in ((a, i), (b, j)):
                rim_copy(chain, step, slab, rim_slot.at[chain, step, slab]).wait_recv()
            total = rim[part, slab, :, :, :, own, :] + rim_slot[a, i, slab] + rim_slot[b, j, slab]
            rim_sum[slab, :, :, 2 * part : 2 * part + 2] = total
        pl.when(has_up)(lambda: far_copy(0, slab).start())
        pl.when(has_down)(lambda: far_copy(1, slab).start())

    takes = jnp.logical_or(jnp.logical_and(z == last, has_down), jnp.logical_and(z == 0, has_up))

    def finish(slab):
        await_fold(slab, z + 1)
        for part in range(2):
            (a, i), (b, j) = ends(part)
            for chain, step in ((a, i), (b, j)):
                main_copy(chain, step, slab, slot.at[chain, step, slab]).wait_recv()
            for p in range(2):
                tiles = local(z + 1, slab, p, part)
                for t in range(2):
                    out_ref[2 * slab + p, :, (2 * part + t) * LANE : (2 * part + t + 1) * LANE] = (
                        tiles[t] + slot[a, i, slab, p, t] + slot[b, j, slab, p, t]
                    )

        @pl.when(takes)
        def _():
            for other in range(depth):
                remote(
                    rim_sum.at[slab, 0], far.at[slab, :, :, other * PIECE : (other + 1) * PIECE, :],
                    far_send.at[slab, 0], far_recv.at[slab, other], (r, c, around(1)),
                ).wait_recv()
            for p in range(2):
                for t in range(4):
                    out_ref[2 * slab + p, :, t * LANE : (t + 1) * LANE] += far[slab, p, t]

    pl.when(jnp.logical_not(has_right))(lambda: took.__setitem__(0, jnp.zeros_like(took[0])))
    pl.when(jnp.logical_not(has_left))(lambda: took.__setitem__(1, jnp.zeros_like(took[1])))

    outward()
    fold(1)
    inward()
    fold(0)
    rim_load(1)
    rim_round(0, 1)
    main_round(0, 1)
    rim_load(0)
    rim_round(0, 0)
    main_round(0, 0)
    rim_round(1, 1)
    rim_round(1, 0)
    main_round(1, 1)
    rim_round(2, 1)
    rim_round(2, 0)
    main_round(1, 0)
    rim_round(3, 1)
    rim_round(3, 0)
    main_round(2, 1)
    rim_end(1)
    rim_end(0)
    main_round(2, 0)
    main_round(3, 1)
    main_round(3, 0)
    finish(1)
    finish(0)

    for copy in sent:
        copy.wait_send()
    for slab in range(2):
        pl.when(has_up)(lambda: far_copy(0, slab).wait_send())
        pl.when(has_down)(lambda: far_copy(1, slab).wait_send())
    for side in range(2):

        @pl.when((has_left, has_right)[side])
        def _():
            for slab in range(2):
                for block in range(blocks):
                    fold_copy(side, slab, block).wait_send()
            for slab in range(2):
                side_copy(1 - side, slab).wait_send()

        @pl.when((has_down, has_up)[side])
        def _():
            for slab in range(2):
                row_copy(side, slab).wait_send()

        @pl.when(live[side])
        def _():
            for at, part, offset, index, slab in corners:
                if at == side:
                    pl.when(targets[part][0])(lambda: corner_copy(side, part, offset, index, slab).wait_send())
            for chain, (_, _, length) in enumerate(CHAINS):
                for step in range(length):
                    for slab in range(2):
                        ring_copy(side, chain, step, slab).wait_send()


def fused_call(sizes, count, corners, field, phase, probe, halves, measured):
    planes, core, _ = field.shape
    depth = sizes[2]
    reach = core + 2 * HALO
    blocks = reach // BLOCK
    f32, bf16 = jnp.float32, jnp.bfloat16
    dma = pltpu.SemaphoreType.DMA
    smem = pl.BlockSpec(memory_space=pltpu.SMEM)
    return pl.pallas_call(
        functools.partial(fused_kernel, sizes),
        out_shape=jax.ShapeDtypeStruct((planes, BLOCK, core), f32),
        in_specs=[smem, smem] + [pl.BlockSpec(memory_space=pltpu.HBM)] * 5,
        out_specs=pl.BlockSpec(memory_space=pltpu.VMEM),
        scratch_shapes=[
            pltpu.VMEM((planes // 2, 6, reach, LANE), f32),
            pltpu.VMEM((planes // 2, 6, reach, LANE), f32),
            pltpu.VMEM((2, PATCH, PATCH), f32),
            pltpu.VMEM((2, PATCH, PATCH), f32),
            pltpu.VMEM((PMAX, PATCH, PATCH), f32),
            pltpu.VMEM((2 * PATCH, 2 * PATCH), bf16),
            pltpu.VMEM((2 * PATCH, 2 * PATCH), bf16),
            pltpu.VMEM((2, PATCH, PATCH), bf16),
            pltpu.VMEM((PMAX, 2 * PATCH, PATCH), bf16),
            pltpu.VMEM((PMAX, planes, 5, PATCH + 2 * BLOCK, LANE), f32),
            pltpu.VMEM((2, 2, blocks, 2, BLOCK // 2, LANE), f32),
            pltpu.VMEM((2, 2, blocks, 2, BLOCK // 2, LANE), f32),
            pltpu.VMEM((4, 2, 2, 2, BLOCK, LANE), f32),
            pltpu.VMEM((2, 2, 2, 2, 2, BLOCK, LANE), f32),
            pltpu.VMEM((4, FAR, 2, 2, 2, 2, PIECE, LANE), f32),
            pltpu.VMEM((4, FAR, 2, 2, 2, BLOCK, LANE), f32),
            pltpu.VMEM((2, 2, 2, 4, PIECE, LANE), f32),
            pltpu.VMEM((2, 2, 4, BLOCK, LANE), f32),
            dma((4,)), dma((2, 4)), dma((2, 2)), dma((2, 2)), dma((2, 4, FAR, 2)), dma((2, 4, FAR, 2)),
            dma((2, 2)), dma((2, 2)), dma((2, 2, depth, 2)), dma((2, 2, depth, 2)),
            dma((2, 2, blocks)), dma((2, 2, blocks)), dma((4, FAR, 2)), dma((4, FAR, 2)),
            dma((4, FAR, 2)), dma((4, FAR, 2)), dma((2, 2)), dma((2, depth)),
        ],
        compiler_params=pltpu.CompilerParams(
            collective_id=0, has_side_effects=True, vmem_limit_bytes=63 << 20
        ),
    )(count, corners, field, phase, probe, halves, measured)


def shards(sizes, object_field, probe_field, prop_phase, measured, positions, counts):
    gradient = fused_call(
        sizes,
        counts.reshape(1),
        positions.reshape(PMAX, 2).T,
        object_field.reshape(4, *object_field.shape[2:]),
        prop_phase,
        probe_field,
        jnp.asarray(dft_halves()),
        measured.reshape(PMAX, PATCH, PATCH),
    )
    return gradient.reshape(2, 2, *gradient.shape[1:])


def solution(mesh):
    placed = (
        P(None, None, "row", "col"),
        P(),
        P(),
        P("row", "col", "scan", None, None, None),
        P("row", "col", "scan", None, None),
        P("row", "col", "scan"),
    )
    sizes = tuple(mesh.shape[name] for name in ("row", "col", "scan"))
    return jax.shard_map(
        functools.partial(shards, sizes),
        mesh=mesh,
        in_specs=placed,
        out_specs=P(None, None, ("row", "scan"), "col"),
        check_vma=False,
    )
```
